512 devices in a mesh: cand: 16 (over y, x), row: 4 (over z_hi), col: 8 (over z_lo, core).
Axes of the slice: x: 4, y: 4, z: 16 (z_hi: 4, z_lo: 4; z = z_hi * 4 + z_lo), core: 2. Of those that a mesh axis runs over, the one named last changes fastest.
Arguments:
- embedding: bfloat16 [1024, 1536], P(('row', 'col')), may hold values from -6 to 6
- bases_table: bfloat16 [4, 1536], replicated, may hold values from -10 to 10
- edit_pos: int32 [1024], P('cand'), parts along dimension 0, may hold values from 0 to 1023
- edit_tok: int32 [1024], P('cand'), parts along dimension 0, may hold values from 0 to 3
- w_row: bfloat16 [1536, 128], replicated, may hold values from -0.15625 to 0.15625
- w_col: bfloat16 [1536, 128], replicated, may hold values from -0.15625 to 0.15625
- dist_gain: float32 [128], replicated, may hold values from -4 to 4
- first_kernel: bfloat16 [3, 3, 128, 128], replicated, may hold values from -0.1875 to 0.1875
- second_kernel: bfloat16 [3, 3, 128, 128], replicated, may hold values from -0.1875 to 0.1875
- head_weight: bfloat16 [128], replicated, may hold values from -0.5 to 0.5
Outputs:
- contact: float32 [4096, 256], P(('cand', 'row'), 'col'), parts along dimension 0
The draws below stay inside these ranges and needn't reach their ends.
There are 16 independent parts, one for each index of `cand`. The reference program is written for one: setup_inputs(seed, part) draws one part's arguments, and reference() takes and returns one part's arrays. A program takes and returns all parts, laid end to end along the dimension named above; an argument that names none is the same for every part. Nothing has to cross between parts.
Inputs may be any that keep to these rules, and one draw needn't show every extreme that they name: `edit_pos`: two substitutions may fall on the same input bin.
All inputs are finite; a program needn't handle non-finite values.
Results may differ from the reference program's by a relative error of at most 0.015.
Values may be sent and summed in bfloat16 or wider, within the bound.
A program may use at most 64 MiB of HBM per device.

```python
import math
import jax
import jax.numpy as jnp
from jax import lax

SEQ_CH = 1536
PAIR_CH = 128
POOL = 4
FIRST_SPACING = 2
SECOND_SPACING = 4
EDITS = 64
BASES = 4
SEQ_BINS = 1024


def plant(result, rng, least, largest):
    dims = result.shape
    index_at = [jax.random.randint(jax.random.fold_in(rng, axis), (), 0, dims[axis]) for axis in range(len(dims))]
    result = result.at[tuple(index_at)].set(least)
    longest = dims.index(max(dims))
    index_at[longest] = (index_at[longest] + 1) % dims[longest]
    return result.at[tuple(index_at)].set(largest)


def levels(stream_key, extent, pieces, low, high):
    loudness, own = 1.0, jax.random.fold_in(stream_key, 6)
    for dim, shards_of in pieces:
        heights = jnp.exp(jax.random.uniform(jax.random.fold_in(own, dim), (shards_of,), jnp.float32, low / len(pieces), high / len(pieces)))
        loudness = loudness * jnp.repeat(heights, extent[dim] // shards_of).reshape([-1 if axis == dim else 1 for axis in range(len(extent))])
    return loudness


def normal_values(key, shape, spread, reach, pieces=(), kind=jnp.bfloat16):
    gain = levels(key, shape, pieces, -0.22, 0.18) if pieces else 1.0
    array = jax.random.normal(key, shape, jnp.float32) * spread * gain
    return jnp.minimum(jnp.maximum(array, -reach), reach).astype(kind)


def setup_inputs(seed: int = 0, part: int = 0) -> dict:
    splits = jax.random.split(jax.random.key(seed), 11)
    part_keys = jax.random.split(jax.random.fold_in(splits[10], part), 11)
    return {
        "embedding": normal_values(splits[0], (SEQ_BINS, SEQ_CH), 1.0, 6.0, ((0, 32),)),
        "bases_table": normal_values(splits[1], (BASES, SEQ_CH), 2.0, 10.0),
        "edit_pos": plant(jax.random.randint(part_keys[2], (EDITS,), 0, SEQ_BINS), jax.random.fold_in(part_keys[2], 1), 0, SEQ_BINS - 1).astype(jnp.int32),
        "edit_tok": plant(jax.random.randint(part_keys[3], (EDITS,), 0, BASES), jax.random.fold_in(part_keys[3], 1), 0, BASES - 1).astype(jnp.int32),
        "w_row": normal_values(splits[4], (SEQ_CH, PAIR_CH), SEQ_CH ** -0.5, 0.15625),
        "w_col": normal_values(splits[5], (SEQ_CH, PAIR_CH), SEQ_CH ** -0.5, 0.15625),
        "dist_gain": normal_values(splits[6], (PAIR_CH,), 1.0, 4.0, (), jnp.float32),
        "first_kernel": normal_values(splits[7], (3, 3, PAIR_CH, PAIR_CH), (9 * PAIR_CH) ** -0.5, 0.1875),
        "second_kernel": normal_values(splits[8], (3, 3, PAIR_CH, PAIR_CH), (9 * PAIR_CH) ** -0.5, 0.1875),
        "head_weight": normal_values(splits[9], (PAIR_CH,), PAIR_CH ** -0.5, 0.5),
    }


def spaced_convolve(features, weight, dilation):
    size = features.shape[0]
    channels = features.shape[2]
    padded = jnp.pad(features, ((dilation, dilation), (dilation, dilation), (0, 0)))
    summed = jnp.zeros((size * size, weight.shape[3]), jnp.float32)
    for a in range(3):
        for b in range(3):
            window = padded[dilation * a:dilation * a + size, dilation * b:dilation * b + size]
            summed = summed + jnp.dot(window.reshape(size * size, channels), weight[a, b], preferred_element_type=jnp.float32)
    return summed.reshape(size, size, weight.shape[3])


def reference(embedding, bases_table, edit_pos, edit_tok, w_row, w_col, dist_gain, first_kernel, second_kernel, head_weight):
    seq_bins = embedding.shape[0]
    channels = embedding.shape[1]
    map_bins = seq_bins // POOL
    edit_delta = jnp.zeros((seq_bins, channels), jnp.float32).at[edit_pos].add(bases_table[edit_tok].astype(jnp.float32))
    edited = embedding.astype(jnp.float32) + edit_delta
    pooled = jnp.mean(edited.reshape(map_bins, POOL, channels), axis=1).astype(jnp.bfloat16)
    row_proj = jnp.dot(pooled, w_row, preferred_element_type=jnp.float32).astype(jnp.bfloat16)
    col_proj = jnp.dot(pooled, w_col, preferred_element_type=jnp.float32).astype(jnp.bfloat16)
    bin_index = jnp.arange(map_bins, dtype=jnp.int32)
    distance = jnp.abs(bin_index[:, None] - bin_index[None, :]).astype(jnp.float32)
    dist_feat = jnp.log1p(distance) * (1.0 / math.log(map_bins))
    pair_grid = jax.nn.relu(row_proj.astype(jnp.float32)[:, None, :] + col_proj.astype(jnp.float32)[None, :, :]
                           + dist_gain[None, None, :] * dist_feat[:, :, None]).astype(jnp.bfloat16)
    first_hidden = (pair_grid.astype(jnp.float32) + jax.nn.relu(spaced_convolve(pair_grid, first_kernel, FIRST_SPACING))).astype(jnp.bfloat16)
    second_hidden = first_hidden.astype(jnp.float32) + jax.nn.relu(spaced_convolve(first_hidden, second_kernel, SECOND_SPACING))
    score = jnp.dot(second_hidden.reshape(map_bins * map_bins, -1), head_weight.astype(jnp.float32),
                    precision=lax.Precision.HIGHEST).reshape(map_bins, map_bins)
    return 0.5 * (score + score.T)
```

```python
import functools
import math

import jax
import jax.numpy as jnp
from jax import lax
from jax.experimental import pallas as pl
from jax.experimental.pallas import tpu as pltpu
from jax.sharding import PartitionSpec as P

MESH = pl.DeviceIdType.MESH
BF16 = jnp.bfloat16
F32 = jnp.float32

ROWS, COLS = 4, 8
GROUP = ROWS * COLS
BINS = 8
POOL = 4
CH = 128
TILE_I, TILE_J = 64, 32
MAP = 256
PITCH = 80
PAIR_J = 44
HID_J = 40
OUTSIDE = -1e30


def kernel(
    emb_h, tab_h, pos_h, tok_h, wr_h, wc_h, gain_h, k1_h, k2_h, hw_h,
    out_ref,
    emb, tab, pos, tok, wr, wc, gain, hw, rhs1, rhs2,
    prow, pcol, rowbuf, colbuf, rowf, colf, table, inside, x1, x2, score, mirror,
    in_sem, send_sem, row_sem, col_sem, swap_send, swap_recv,
):
    r = lax.axis_index("row")
    c = lax.axis_index("col")
    g = r * COLS + c

    def load(src, dst, k):
        copy = pltpu.make_async_copy(src, dst, in_sem.at[k])
        copy.start()
        return copy

    first = [
        load(emb_h, emb, 0), load(tab_h, tab, 1), load(pos_h, pos, 2), load(tok_h, tok, 3),
        load(wr_h, wr, 4), load(wc_h, wc, 5),
    ]
    later = [load(gain_h, gain, 6), load(hw_h, hw, 7)]
    for b in range(3):
        later.append(load(k1_h.at[:, b], rhs1.at[b, :, :, pl.ds(0, CH)], 8 + b))
        later.append(load(k1_h.at[:, b], rhs1.at[b + 1, :, :, pl.ds(CH, CH)], 11 + b))
    last = []
    for b in range(3):
        last.append(load(k2_h.at[:, b], rhs2.at[b, :, :, pl.ds(0, CH)], 14 + b))
        last.append(load(k2_h.at[:, b], rhs2.at[b + 1, :, :, pl.ds(CH, CH)], 17 + b))

    barrier = pltpu.get_barrier_semaphore()
    for k in range(1, GROUP):
        other = lax.rem(g + k, GROUP)
        pl.semaphore_signal(
            barrier, inc=1, device_id={"row": other // COLS, "col": lax.rem(other, COLS)}, device_id_type=MESH
        )

    blank = jnp.zeros((3, CH, CH), BF16)
    for rhs in (rhs1, rhs2):
        rhs[3, :, :, pl.ds(0, CH)] = blank
        rhs[0, :, :, pl.ds(CH, CH)] = blank

    for copy in first:
        copy.wait()
    own = lax.shift_right_logical(pos[...], 2) == g * BINS + lax.broadcasted_iota(jnp.int32, (BINS, 64), 0)
    token = jnp.broadcast_to(tok[...], (BINS, 64))
    pool = (
        lax.broadcasted_iota(jnp.int32, (BINS, 32), 1) // POOL == lax.broadcasted_iota(jnp.int32, (BINS, 32), 0)
    ).astype(BF16)
    total = jnp.dot(pool, emb[...], preferred_element_type=F32)
    bases = tab[...].astype(F32)
    for t in range(4):
        count = jnp.sum(jnp.where(own & (token == t), 1.0, 0.0), axis=1, keepdims=True)
        total = total + count * bases[t : t + 1, :]
    pooled = (total * (1.0 / POOL)).astype(BF16)
    prow[...] = jnp.dot(pooled, wr[...], preferred_element_type=F32).astype(BF16)
    pcol[...] = jnp.dot(pooled, wc[...], preferred_element_type=F32).astype(BF16)

    pl.semaphore_wait(barrier, GROUP - 1)

    def send(src, dst, ssem, rsem, row, col):
        return pltpu.make_async_remote_copy(
            src_ref=src, dst_ref=dst, send_sem=ssem, recv_sem=rsem,
            device_id={"row": row, "col": col}, device_id_type=MESH,
        )

    up = lax.rem(r + ROWS - 1, ROWS)
    down = lax.rem(r + 1, ROWS)
    mine = g // 4
    part = lax.rem(g, 4)
    left = lax.rem(mine + COLS - 1, COLS)
    right = lax.rem(mine + 1, COLS)

    def row_send(k, slot, row, col):
        return send(prow, rowbuf.at[slot], send_sem.at[k], row_sem.at[slot], row, col)

    def col_send(k, slot, row, col):
        return send(pcol, colbuf.at[slot], send_sem.at[k], col_sem.at[slot], row, col)

    def every_send(do):
        for k in range(1, COLS):
            do(row_send(k, c + 1, r, lax.rem(c + k, COLS)))
        for k in range(1, ROWS):
            do(col_send(7 + k, part + 1, lax.rem(r + k, ROWS), mine))

        @pl.when(c != mine)
        def _():
            do(col_send(11, part + 1, r, mine))

        @pl.when(c == 0)
        def _():
            for k in range(COLS):
                do(row_send(12 + k, 9, up, k))

        @pl.when(c == COLS - 1)
        def _():
            for k in range(COLS):
                do(row_send(12 + k, 0, down, k))

        @pl.when(part == 0)
        def _():
            for k in range(1, ROWS):
                do(col_send(20 + k, 5, lax.rem(r + k, ROWS), left))

            @pl.when(c != left)
            def _():
                do(col_send(24, 5, r, left))

        @pl.when(part == 3)
        def _():
            for k in range(1, ROWS):
                do(col_send(20 + k, 0, lax.rem(r + k, ROWS), right))

            @pl.when(c != right)
            def _():
                do(col_send(24, 0, r, right))

    every_send(lambda copy: copy.start())

    rowbuf[c + 1] = prow[...]

    @pl.when(c == mine)
    def _():
        colbuf[part + 1] = pcol[...]

    @pl.when((part == 0) & (c == left))
    def _():
        colbuf[5] = pcol[...]

    @pl.when((part == 3) & (c == right))
    def _():
        colbuf[0] = pcol[...]

    for copy in later:
        copy.wait()
    offset = (TILE_I * r - TILE_J * c - 47 + lax.broadcasted_iota(jnp.int32, (128, CH), 0)).astype(F32)
    table[...] = gain[...] * (jnp.log(1.0 + jnp.abs(offset)) * (1.0 / math.log(MAP)))
    bin_i = TILE_I * r - 8 + lax.broadcasted_iota(jnp.int32, (PITCH, CH), 0)
    in_i = (bin_i >= 0) & (bin_i < MAP)
    inside[...] = in_i.astype(F32)
    bin_j = TILE_J * c - 8 + lax.broadcasted_iota(jnp.int32, (48, CH), 0)
    in_j = (bin_j >= 0) & (bin_j < MAP)
    rowf[pl.ds(0, 8), :] = jnp.full((8, CH), OUTSIDE, F32)
    rowf[pl.ds(88, 8), :] = jnp.full((8, CH), OUTSIDE, F32)

    def arrived(buf, slot, sem):
        pltpu.make_async_copy(buf.at[slot], buf.at[slot], sem.at[slot]).wait()

    for k in range(1, COLS):
        arrived(rowbuf, 1 + lax.rem(c + k, COLS), row_sem)
    arrived(rowbuf, 0, row_sem)
    arrived(rowbuf, 9, row_sem)
    for k in range(6):
        origin = lax.rem(4 * c - 1 + k + GROUP, GROUP)

        @pl.when(origin != g)
        def _():
            arrived(colbuf, k, col_sem)

    rowf[pl.ds(8, PITCH), :] = jnp.where(in_i, rowbuf[...].astype(F32).reshape(PITCH, CH), OUTSIDE)
    colf[...] = jnp.where(in_j, colbuf[...].astype(F32).reshape(48, CH), OUTSIDE)

    for p in range(PAIR_J):
        column = colf[pl.ds(p + 2, 1), :]
        for a in range(3):
            move = 2 * (a - 1)
            value = rowf[pl.ds(8 + move, PITCH), :] + column + table[pl.ds(45 - p + move, PITCH), :]
            x1[p, :, pl.ds(a * CH, CH)] = jnp.maximum(value, 0.0).astype(BF16)

    w1 = rhs1[...].reshape(12 * CH, 2 * CH)

    def first_conv(n, carry):
        q0 = 8 * n
        starts = (0, 1, 4, 5)
        lhs = jnp.concatenate(
            [jnp.concatenate([x1[q0 + s + 2 * m] for m in range(4)], axis=1) for s in starts], axis=0
        )
        acc = jnp.dot(lhs, rhs1[...].reshape(12 * CH, 2 * CH), preferred_element_type=F32)
        for k, s in enumerate(starts):
            for half in range(2):
                q = q0 + s + 2 * half
                j = TILE_J * c - 4 + q
                scale = jnp.where((j >= 0) & (j < MAP), 1.0, 0.0)
                conv = acc[PITCH * k : PITCH * (k + 1), CH * half : CH * (half + 1)]
                base = x1[q + 2, :, pl.ds(CH, CH)].astype(F32)
                hidden = base + jnp.maximum(conv, 0.0) * (inside[...] * scale)
                for a in range(3):
                    x2[q, :, pl.ds(a * CH, CH)] = hidden[4 + 4 * a : 68 + 4 * a].astype(BF16)
        return carry

    lax.fori_loop(0, HID_J // 8, first_conv, 0)

    for copy in last:
        copy.wait()
    head = jnp.concatenate([jnp.broadcast_to(hw[...].astype(F32), (CH, CH)).T.astype(BF16)] * 2, axis=0)
    lane = lax.broadcasted_iota(jnp.int32, (TILE_I, CH), 1) - TILE_J * lax.rem(c, 2)

    def second_conv(n, total):
        t0 = 8 * n
        lhs = jnp.concatenate(
            [jnp.concatenate([x2[t0 + s + 4 * m] for m in range(4)], axis=1) for s in range(4)], axis=0
        )
        acc = jnp.dot(lhs, rhs2[...].reshape(12 * CH, 2 * CH), preferred_element_type=F32)
        pieces = []
        for half in range(2):
            for s in range(4):
                conv = acc[TILE_I * s : TILE_I * (s + 1), CH * half : CH * (half + 1)]
                base = x2[t0 + s + 4 * half + 4, :, pl.ds(CH, CH)].astype(F32)
                hidden = base + jnp.maximum(conv, 0.0)
                high = hidden.astype(BF16)
                low = (hidden - high.astype(F32)).astype(BF16)
                pieces.append(jnp.concatenate([high, low], axis=1))
        points = jnp.dot(jnp.concatenate(pieces, axis=0), head, preferred_element_type=F32)
        for k in range(8):
            total = jnp.where(lane == t0 + k, points[TILE_I * k : TILE_I * (k + 1)], total)
        return total

    total = lax.fori_loop(0, TILE_J // 8, second_conv, jnp.zeros((TILE_I, CH), F32))
    score[...] = total.reshape(2, TILE_J, CH)

    side = lax.rem(c, 2)
    swaps = [
        send(score.at[h], mirror.at[side], swap_send.at[h], swap_recv.at[side], c // 2, 2 * r + h) for h in range(2)
    ]
    diagonal = c // 2 == r
    for h in range(2):
        here = diagonal & (side == h)

        @pl.when(jnp.logical_not(here))
        def _():
            swaps[h].start()

        @pl.when(here)
        def _():
            mirror[side] = score[h]

    turned = total.T
    table[:, pl.ds(0, TILE_I)] = turned
    every_send(lambda copy: copy.wait_send())
    for h in range(2):
        @pl.when(jnp.logical_not(diagonal & (side == h)))
        def _():
            pltpu.make_async_copy(mirror.at[h], mirror.at[h], swap_recv.at[h]).wait()
            swaps[h].wait_send()

    straight = table[pl.ds(pl.multiple_of(TILE_J * side, TILE_J), TILE_J), pl.ds(0, TILE_I)]
    out_ref[...] = 0.5 * (straight + (mirror[0] + mirror[1])[:, :TILE_I])


def on_device(embedding, bases_table, edit_pos, edit_tok, w_row, w_col, dist_gain, first_kernel, second_kernel, head_weight):
    channels = embedding.shape[1]
    anywhere = pl.BlockSpec(memory_space=pltpu.HBM)
    turned = pl.pallas_call(
        kernel,
        out_shape=jax.ShapeDtypeStruct((TILE_J, TILE_I), F32),
        in_specs=[anywhere] * 10,
        out_specs=pl.BlockSpec(memory_space=pltpu.VMEM),
        scratch_shapes=[
            pltpu.VMEM((32, channels), BF16),
            pltpu.VMEM((4, channels), BF16),
            pltpu.VMEM((1, 64), jnp.int32),
            pltpu.VMEM((1, 64), jnp.int32),
            pltpu.VMEM((channels, CH), BF16),
            pltpu.VMEM((channels, CH), BF16),
            pltpu.VMEM((1, CH), F32),
            pltpu.VMEM((1, CH), BF16),
            pltpu.VMEM((4, 3, CH, 2 * CH), BF16),
            pltpu.VMEM((4, 3, CH, 2 * CH), BF16),
            pltpu.VMEM((BINS, CH), BF16),
            pltpu.VMEM((BINS, CH), BF16),
            pltpu.VMEM((10, BINS, CH), BF16),
            pltpu.VMEM((6, BINS, CH), BF16),
            pltpu.VMEM((96, CH), F32),
            pltpu.VMEM((48, CH), F32),
            pltpu.VMEM((128, CH), F32),
            pltpu.VMEM((PITCH, CH), F32),
            pltpu.VMEM((PAIR_J, PITCH, 3 * CH), BF16),
            pltpu.VMEM((HID_J, TILE_I, 3 * CH), BF16),
            pltpu.VMEM((2, TILE_J, CH), F32),
            pltpu.VMEM((2, TILE_J, CH), F32),
            pltpu.SemaphoreType.DMA((20,)),
            pltpu.SemaphoreType.DMA((25,)),
            pltpu.SemaphoreType.DMA((10,)),
            pltpu.SemaphoreType.DMA((6,)),
            pltpu.SemaphoreType.DMA((2,)),
            pltpu.SemaphoreType.DMA((2,)),
        ],
        compiler_params=pltpu.CompilerParams(
            collective_id=0, has_side_effects=True, vmem_limit_bytes=40 * 1024 * 1024
        ),
    )(
        embedding, bases_table, edit_pos.reshape(1, -1), edit_tok.reshape(1, -1), w_row, w_col,
        dist_gain.reshape(1, -1), first_kernel, second_kernel, head_weight.reshape(1, -1),
    )
    return turned.T


def solution(mesh):
    placed = (P(("row", "col"), None), P(), P("cand"), P("cand"), P(), P(), P(), P(), P(), P())
    return jax.shard_map(
        on_device, mesh=mesh, in_specs=placed, out_specs=P(("cand", "row"), "col"), check_vma=False
    )
```

```python
import functools
import math

import jax
import jax.numpy as jnp
from jax import lax
from jax.experimental import pallas as pl
from jax.experimental.pallas import tpu as pltpu
from jax.sharding import PartitionSpec as P

MESH = pl.DeviceIdType.MESH
BF16 = jnp.bfloat16
F32 = jnp.float32

ROWS, COLS = 4, 8
GROUP = ROWS * COLS
BINS = 8
POOL = 4
CH = 128
TILE_I, TILE_J = 64, 32
MAP = 256
PITCH = 80
PAIR_J = 44
HID_J = 40
OUTSIDE = -1e30


def kernel(
    emb_h, tab_h, pos_h, tok_h, wr_h, wc_h, gain_h, k1_h, k2_h, hw_h,
    out_ref,
    emb, tab, pos, tok, wr, wc, gain, hw, rhs1, rhs2,
    prow, pcol, rowbuf, colbuf, rowf, colf, table, inside, x1, x2, score, mirror,
    in_sem, send_sem, row_sem, col_sem, swap_send, swap_recv,
):
    r = lax.axis_index("row")
    c = lax.axis_index("col")
    g = r * COLS + c

    def load(src, dst, k):
        copy = pltpu.make_async_copy(src, dst, in_sem.at[k])
        copy.start()
        return copy

    first = [
        load(emb_h, emb, 0), load(tab_h, tab, 1), load(pos_h, pos, 2), load(tok_h, tok, 3),
        load(wr_h, wr, 4), load(wc_h, wc, 5),
    ]
    later = [load(gain_h, gain, 6), load(hw_h, hw, 7)]
    for b in range(3):
        later.append(load(k1_h.at[:, b], rhs1.at[b, :, :, pl.ds(0, CH)], 8 + b))
        later.append(load(k1_h.at[:, b], rhs1.at[b + 1, :, :, pl.ds(CH, CH)], 11 + b))
    last = []
    for b in range(3):
        last.append(load(k2_h.at[:, b], rhs2.at[b, :, :, pl.ds(0, CH)], 14 + b))
        last.append(load(k2_h.at[:, b], rhs2.at[b + 1, :, :, pl.ds(CH, CH)], 17 + b))

    barrier = pltpu.get_barrier_semaphore()
    for k in range(1, GROUP):
        other = lax.rem(g + k, GROUP)
        pl.semaphore_signal(
            barrier, inc=1, device_id={"row": other // COLS, "col": lax.rem(other, COLS)}, device_id_type=MESH
        )

    blank = jnp.zeros((3, CH, CH), BF16)
    for rhs in (rhs1, rhs2):
        rhs[3, :, :, pl.ds(0, CH)] = blank
        rhs[0, :, :, pl.ds(CH, CH)] = blank

    for copy in first:
        copy.wait()
    own = lax.shift_right_logical(pos[...], 2) == g * BINS + lax.broadcasted_iota(jnp.int32, (BINS, 64), 0)
    token = jnp.broadcast_to(tok[...], (BINS, 64))
    pool = (
        lax.broadcasted_iota(jnp.int32, (BINS, 32), 1) // POOL == lax.broadcasted_iota(jnp.int32, (BINS, 32), 0)
    ).astype(BF16)
    total = jnp.dot(pool, emb[...], preferred_element_type=F32)
    bases = tab[...].astype(F32)
    for t in range(4):
        count = jnp.sum(jnp.where(own & (token == t), 1.0, 0.0), axis=1, keepdims=True)
        total = total + count * bases[t : t + 1, :]
    pooled = (total * (1.0 / POOL)).astype(BF16)
    prow[...] = jnp.dot(pooled, wr[...], preferred_element_type=F32).astype(BF16)
    pcol[...] = jnp.dot(pooled, wc[...], preferred_element_type=F32).astype(BF16)

    pl.semaphore_wait(barrier, GROUP - 1)

    def send(src, dst, ssem, rsem, row, col):
        return pltpu.make_async_remote_copy(
            src_ref=src, dst_ref=dst, send_sem=ssem, recv_sem=rsem,
            device_id={"row": row, "col": col}, device_id_type=MESH,
        )

    up = lax.rem(r + ROWS - 1, ROWS)
    down = lax.rem(r + 1, ROWS)
    mine = g // 4
    part = lax.rem(g, 4)
    left = lax.rem(mine + COLS - 1, COLS)
    right = lax.rem(mine + 1, COLS)

    def row_send(k, slot, row, col):
        return send(prow, rowbuf.at[slot], send_sem.at[k], row_sem.at[slot], row, col)

    def col_send(k, slot, row, col):
        return send(pcol, colbuf.at[slot], send_sem.at[k], col_sem.at[slot], row, col)

    def every_send(do):
        for k in range(1, COLS):
            do(row_send(k, c + 1, r, lax.rem(c + k, COLS)))
        for k in range(1, ROWS):
            do(col_send(7 + k, part + 1, lax.rem(r + k, ROWS), mine))

        @pl.when(c != mine)
        def _():
            do(col_send(11, part + 1, r, mine))

        @pl.when(c == 0)
        def _():
            for k in range(COLS):
                do(row_send(12 + k, 9, up, k))

        @pl.when(c == COLS - 1)
        def _():
            for k in range(COLS):
                do(row_send(12 + k, 0, down, k))

        @pl.when(part == 0)
        def _():
            for k in range(1, ROWS):
                do(col_send(20 + k, 5, lax.rem(r + k, ROWS), left))

            @pl.when(c != left)
            def _():
                do(col_send(24, 5, r, left))

        @pl.when(part == 3)
        def _():
            for k in range(1, ROWS):
                do(col_send(20 + k, 0, lax.rem(r + k, ROWS), right))

            @pl.when(c != right)
            def _():
                do(col_send(24, 0, r, right))

    every_send(lambda copy: copy.start())

    rowbuf[c + 1] = prow[...]

    @pl.when(c == mine)
    def _():
        colbuf[part + 1] = pcol[...]

    @pl.when((part == 0) & (c == left))
    def _():
        colbuf[5] = pcol[...]

    @pl.when((part == 3) & (c == right))
    def _():
        colbuf[0] = pcol[...]

    for copy in later:
        copy.wait()
    offset = (TILE_I * r - TILE_J * c - 47 + lax.broadcasted_iota(jnp.int32, (128, CH), 0)).astype(F32)
    table[...] = gain[...] * (jnp.log(1.0 + jnp.abs(offset)) * (1.0 / math.log(MAP)))
    bin_i = TILE_I * r - 8 + lax.broadcasted_iota(jnp.int32, (PITCH, CH), 0)
    in_i = (bin_i >= 0) & (bin_i < MAP)
    inside[...] = in_i.astype(F32)
    bin_j = TILE_J * c - 8 + lax.broadcasted_iota(jnp.int32, (48, CH), 0)
    in_j = (bin_j >= 0) & (bin_j < MAP)
    rowf[pl.ds(0, 8), :] = jnp.full((8, CH), OUTSIDE, F32)
    rowf[pl.ds(88, 8), :] = jnp.full((8, CH), OUTSIDE, F32)

    def arrived(buf, slot, sem):
        pltpu.make_async_copy(buf.at[slot], buf.at[slot], sem.at[slot]).wait()

    for k in range(1, COLS):
        arrived(rowbuf, 1 + lax.rem(c + k, COLS), row_sem)
    arrived(rowbuf, 0, row_sem)
    arrived(rowbuf, 9, row_sem)
    for k in range(6):
        origin = lax.rem(4 * c - 1 + k + GROUP, GROUP)

        @pl.when(origin != g)
        def _():
            arrived(colbuf, k, col_sem)

    rowf[pl.ds(8, PITCH), :] = jnp.where(in_i, rowbuf[...].astype(F32).reshape(PITCH, CH), OUTSIDE)
    colf[...] = jnp.where(in_j, colbuf[...].astype(F32).reshape(48, CH), OUTSIDE)

    for p in range(PAIR_J):
        column = colf[pl.ds(p + 2, 1), :]
        for a in range(3):
            move = 2 * (a - 1)
            value = rowf[pl.ds(8 + move, PITCH), :] + column + table[pl.ds(45 - p + move, PITCH), :]
            x1[p, :, pl.ds(a * CH, CH)] = jnp.maximum(value, 0.0).astype(BF16)

    w1 = rhs1[...].reshape(12 * CH, 2 * CH)

    def first_conv(n, carry):
        q0 = 8 * n
        starts = (0, 1, 4, 5)
        lhs = jnp.concatenate(
            [jnp.concatenate([x1[q0 + s + 2 * m] for m in range(4)], axis=1) for s in starts], axis=0
        )
        acc = jnp.dot(lhs, rhs1[...].reshape(12 * CH, 2 * CH), preferred_element_type=F32)
        for k, s in enumerate(starts):
            for half in range(2):
                q = q0 + s + 2 * half
                j = TILE_J * c - 4 + q
                scale = jnp.where((j >= 0) & (j < MAP), 1.0, 0.0)
                conv = acc[PITCH * k : PITCH * (k + 1), CH * half : CH * (half + 1)]
                base = x1[q + 2, :, pl.ds(CH, CH)].astype(F32)
                hidden = base + jnp.maximum(conv, 0.0) * (inside[...] * scale)
                for a in range(3):
                    x2[q, :, pl.ds(a * CH, CH)] = hidden[4 + 4 * a : 68 + 4 * a].astype(BF16)
        return carry

    lax.fori_loop(0, HID_J // 8, first_conv, 0)

    for copy in last:
        copy.wait()
    head = jnp.concatenate([jnp.broadcast_to(hw[...].astype(F32), (CH, CH)).T.astype(BF16)] * 2, axis=0)
    lane = lax.broadcasted_iota(jnp.int32, (TILE_I, CH), 1) - TILE_J * lax.rem(c, 2)

    def second_conv(n, total):
        t0 = 8 * n
        lhs = jnp.concatenate(
            [jnp.concatenate([x2[t0 + s + 4 * m] for m in range(4)], axis=1) for s in range(4)], axis=0
        )
        acc = jnp.dot(lhs, rhs2[...].reshape(12 * CH, 2 * CH), preferred_element_type=F32)
        pieces = []
        for half in range(2):
            for s in range(4):
                conv = acc[TILE_I * s : TILE_I * (s + 1), CH * half : CH * (half + 1)]
                base = x2[t0 + s + 4 * half + 4, :, pl.ds(CH, CH)].astype(F32)
                hidden = base + jnp.maximum(conv, 0.0)
                high = hidden.astype(BF16)
                low = (hidden - high.astype(F32)).astype(BF16)
                pieces.append(jnp.concatenate([high, low], axis=1))
        points = jnp.dot(jnp.concatenate(pieces, axis=0), head, preferred_element_type=F32)
        for k in range(8):
            total = jnp.where(lane == t0 + k, points[TILE_I * k : TILE_I * (k + 1)], total)
        return total

    total = lax.fori_loop(0, TILE_J // 8, second_conv, jnp.zeros((TILE_I, CH), F32))
    score[...] = total.reshape(2, TILE_J, CH)

    side = lax.rem(c, 2)
    swaps = [
        send(score.at[h], mirror.at[side], swap_send.at[h], swap_recv.at[side], c // 2, 2 * r + h) for h in range(2)
    ]
    diagonal = c // 2 == r
    for h in range(2):
        here = diagonal & (side == h)

        @pl.when(jnp.logical_not(here))
        def _():
            swaps[h].start()

        @pl.when(here)
        def _():
            mirror[side] = score[h]

    turned = total.T
    table[:, pl.ds(0, TILE_I)] = turned
    every_send(lambda copy: copy.wait_send())
    for h in range(2):
        @pl.when(jnp.logical_not(diagonal & (side == h)))
        def _():
            pltpu.make_async_copy(mirror.at[h], mirror.at[h], swap_recv.at[h]).wait()
            swaps[h].wait_send()

    straight = table[pl.ds(pl.multiple_of(TILE_J * side, TILE_J), TILE_J), pl.ds(0, TILE_I)]
    out_ref[...] = 0.5 * (straight + (mirror[0] + mirror[1])[:, :TILE_I])


def on_device(embedding, bases_table, edit_pos, edit_tok, w_row, w_col, dist_gain, first_kernel, second_kernel, head_weight):
    channels = embedding.shape[1]
    anywhere = pl.BlockSpec(memory_space=pltpu.HBM)
    turned = pl.pallas_call(
        kernel,
        out_shape=jax.ShapeDtypeStruct((TILE_J, TILE_I), F32),
        in_specs=[anywhere] * 10,
        out_specs=pl.BlockSpec(memory_space=pltpu.VMEM),
        scratch_shapes=[
            pltpu.VMEM((32, channels), BF16),
            pltpu.VMEM((4, channels), BF16),
            pltpu.VMEM((1, 64), jnp.int32),
            pltpu.VMEM((1, 64), jnp.int32),
            pltpu.VMEM((channels, CH), BF16),
            pltpu.VMEM((channels, CH), BF16),
            pltpu.VMEM((1, CH), F32),
            pltpu.VMEM((1, CH), BF16),
            pltpu.VMEM((4, 3, CH, 2 * CH), BF16),
            pltpu.VMEM((4, 3, CH, 2 * CH), BF16),
            pltpu.VMEM((BINS, CH), BF16),
            pltpu.VMEM((BINS, CH), BF16),
            pltpu.VMEM((10, BINS, CH), BF16),
            pltpu.VMEM((6, BINS, CH), BF16),
            pltpu.VMEM((96, CH), F32),
            pltpu.VMEM((48, CH), F32),
            pltpu.VMEM((128, CH), F32),
            pltpu.VMEM((PITCH, CH), F32),
            pltpu.VMEM((PAIR_J, PITCH, 3 * CH), BF16),
            pltpu.VMEM((HID_J, TILE_I, 3 * CH), BF16),
            pltpu.VMEM((2, TILE_J, CH), F32),
            pltpu.VMEM((2, TILE_J, CH), F32),
            pltpu.SemaphoreType.DMA((20,)),
            pltpu.SemaphoreType.DMA((25,)),
            pltpu.SemaphoreType.DMA((10,)),
            pltpu.SemaphoreType.DMA((6,)),
            pltpu.SemaphoreType.DMA((2,)),
            pltpu.SemaphoreType.DMA((2,)),
        ],
        compiler_params=pltpu.CompilerParams(
            collective_id=0, has_side_effects=True, vmem_limit_bytes=60 * 1000 * 1000
        ),
    )(
        embedding, bases_table, edit_pos.reshape(1, -1), edit_tok.reshape(1, -1), w_row, w_col,
        dist_gain.reshape(1, -1), first_kernel, second_kernel, head_weight.reshape(1, -1),
    )
    return turned.T


def solution(mesh):
    placed = (P(("row", "col"), None), P(), P("cand"), P("cand"), P(), P(), P(), P(), P(), P())
    return jax.shard_map(
        on_device, mesh=mesh, in_specs=placed, out_specs=P(("cand", "row"), "col"), check_vma=False
    )
```

```python
import math

import jax
import jax.numpy as jnp
from jax import lax
from jax.experimental import pallas as pl
from jax.experimental.pallas import tpu as pltpu
from jax.sharding import PartitionSpec as P

MESH = pl.DeviceIdType.MESH
BF16 = jnp.bfloat16
F32 = jnp.float32

ROWS, COLS = 4, 8
BINS = 8
POOL = 4
CH = 128
TILE_I, TILE_J = 64, 32
MAP = 256
PITCH = 80
PAIR_J = 44
HID_J = 40
OUTSIDE = -1e30


def kernel(
    emb_h, tab_h, pos_h, tok_h, wr_h, wc_h, gain_h, k1_h, k2_h, hw_h,
    out_ref,
    emb, tab, pos, tok, wr, wc, gain, hw, rhs1, rhs2,
    proj, ibuf, jbuf, fi, fj, table, inside, x1, x2,
    in_sem, send_sem, i_sem, j_sem, block_sem,
):
    r = lax.axis_index("row")
    c = lax.axis_index("col")
    g = r * COLS + c
    mine, part = g // 4, lax.rem(g, 4)
    left, right = mine - 1, mine + 1
    home = c // 2

    barrier = pltpu.get_barrier_semaphore()

    def tell(row, col):
        pl.semaphore_signal(barrier, inc=1, device_id={"row": row, "col": col}, device_id_type=MESH)

    @pl.when(home > r)
    def _():
        for k in range(5):
            tell((4 * c - 1 + k) // COLS, lax.rem(4 * c - 1 + k, COLS))

    @pl.when((home > r) & (c < COLS - 1))
    def _():
        tell((4 * c + 4) // COLS, lax.rem(4 * c + 4, COLS))

    @pl.when(r > 0)
    def _():
        tell(r - 1, COLS - 1)

    @pl.when(r < ROWS - 1)
    def _():
        tell(r + 1, 0)

    for k in range(1, COLS):
        tell(r, lax.rem(c + k, COLS))

    @pl.when(home < r)
    def _():
        tell(home, c)

    def load(src, dst, k):
        copy = pltpu.make_async_copy(src, dst, in_sem.at[k])
        copy.start()
        return copy

    first = [
        load(wr_h, wr, 0), load(wc_h, wc, 1), load(emb_h, emb, 2), load(tab_h, tab, 3), load(pos_h, pos, 4),
        load(tok_h, tok, 5),
    ]
    later = [load(gain_h, gain, 6), load(hw_h, hw, 7)]
    for n, (source, rhs) in enumerate(((k1_h, rhs1), (k2_h, rhs2))):
        for b in range(3):
            for tile, taps in ((0, source.at[:, b]), (1, source.at[b])):
                at = 8 + 12 * n + 4 * b + 2 * tile
                later.append(load(taps, rhs.at[tile, b, :, :, pl.ds(0, CH)], at))
                later.append(load(taps, rhs.at[tile, b + 1, :, :, pl.ds(CH, CH)], at + 1))

    for copy in first:
        copy.wait()
    own = lax.shift_right_logical(pos[...], 2) == g * BINS + lax.broadcasted_iota(jnp.int32, (BINS, 64), 0)
    token = jnp.broadcast_to(tok[...], (BINS, 64))
    pool = (
        lax.broadcasted_iota(jnp.int32, (BINS, 32), 1) // POOL == lax.broadcasted_iota(jnp.int32, (BINS, 32), 0)
    ).astype(BF16)
    total = jnp.dot(pool, emb[...], preferred_element_type=F32)
    bases = tab[...].astype(F32)
    for t in range(4):
        count = jnp.sum(jnp.where(own & (token == t), 1.0, 0.0), axis=1, keepdims=True)
        total = total + count * bases[t : t + 1, :]
    pooled = (total * (1.0 / POOL)).astype(BF16)
    proj[:, pl.ds(0, CH)] = jnp.dot(pooled, wr[...], preferred_element_type=F32).astype(BF16)
    proj[:, pl.ds(CH, CH)] = jnp.dot(pooled, wc[...], preferred_element_type=F32).astype(BF16)

    has_left = (part == 0) & (mine > 0)
    has_right = (part == 3) & (mine < COLS - 1)
    is_top = (c == 0) & (r > 0)
    is_bottom = (c == COLS - 1) & (r < ROWS - 1)
    pl.semaphore_wait(
        barrier,
        COLS - 1 + r
        + jnp.where(has_left, left // 2, 0) + jnp.where(has_right, right // 2, 0)
        + jnp.where(is_top | is_bottom, COLS, 0) + jnp.where(home == r, ROWS - 1 - r, 0),
    )

    def send(src, dst, k, rsem, row, col):
        return pltpu.make_async_remote_copy(
            src_ref=src, dst_ref=dst, send_sem=send_sem.at[k], recv_sem=rsem,
            device_id={"row": row, "col": col}, device_id_type=MESH,
        )

    def i_send(k, slot, row, col):
        return send(proj, ibuf.at[slot], k, i_sem.at[slot], row, col)

    def j_send(k, slot, row, col):
        return send(proj, jbuf.at[slot], k, j_sem.at[slot], row, col)

    def every_send(do):
        for row in range(ROWS - 1):
            @pl.when(row < r)
            def _():
                do(j_send(row, part + 1, row, mine))

        for row in range(ROWS - 1):
            @pl.when(has_left & (row < left // 2))
            def _():
                do(j_send(3 + row, 5, row, left))

        for row in range(ROWS - 1):
            @pl.when(has_right & (row < right // 2))
            def _():
                do(j_send(3 + row, 0, row, right))

        @pl.when(is_top)
        def _():
            for k in range(COLS):
                do(i_send(6 + k, 9, r - 1, k))

        @pl.when(is_bottom)
        def _():
            for k in range(COLS):
                do(i_send(6 + k, 0, r + 1, k))

        for k in range(1, COLS):
            do(i_send(13 + k, c + 1, r, lax.rem(c + k, COLS)))

    def every_forward(do):
        for row in range(1, ROWS):
            @pl.when((home == r) & (row > r))
            def _():
                block = ibuf.at[pl.ds(4 * lax.rem(c, 2), 6)]
                do(send(block, jbuf, 20 + row, block_sem.at[0], row, c))

    every_send(lambda copy: copy.start())

    ibuf[c + 1] = proj[...]
    nothing = jnp.zeros((BINS, 2 * CH), BF16)

    @pl.when(r == 0)
    def _():
        ibuf[0] = nothing

    @pl.when(r == ROWS - 1)
    def _():
        ibuf[9] = nothing

    @pl.when((c == COLS - 1) & (home > r))
    def _():
        jbuf[5] = nothing

    blank = jnp.zeros((3, CH, CH), BF16)
    for rhs in (rhs1, rhs2):
        for tile in range(2):
            rhs[tile, 3, :, :, pl.ds(0, CH)] = blank
            rhs[tile, 0, :, :, pl.ds(CH, CH)] = blank
    for copy in later:
        copy.wait()
    offset = (TILE_I * r - TILE_J * c - 47 + lax.broadcasted_iota(jnp.int32, (128, CH), 0)).astype(F32)
    table[...] = gain[...] * (jnp.log(1.0 + jnp.abs(offset)) * (1.0 / math.log(MAP)))
    bin_i = TILE_I * r - 8 + lax.broadcasted_iota(jnp.int32, (PITCH, CH), 0)
    inside[...] = ((bin_i >= 0) & (bin_i < MAP)).astype(F32)
    fi[pl.ds(0, 8), :] = jnp.full((8, 2 * CH), OUTSIDE, F32)
    fi[pl.ds(88, 8), :] = jnp.full((8, 2 * CH), OUTSIDE, F32)
    head = jnp.concatenate([jnp.broadcast_to(hw[...].astype(F32), (CH, CH)).T.astype(BF16)] * 2, axis=0)
    lane = lax.broadcasted_iota(jnp.int32, (TILE_I, CH), 1)

    def arrived(buf, slot, sem):
        pltpu.make_async_copy(buf.at[slot], buf.at[slot], sem.at[slot]).wait()

    for k in range(1, COLS):
        arrived(ibuf, 1 + lax.rem(c + k, COLS), i_sem)

    @pl.when(r > 0)
    def _():
        arrived(ibuf, 0, i_sem)

    @pl.when(r < ROWS - 1)
    def _():
        arrived(ibuf, 9, i_sem)

    every_forward(lambda copy: copy.start())

    def fill(out, at, block, start, size):
        bins = start + lax.broadcasted_iota(jnp.int32, (size, 2 * CH), 0)
        values = block.astype(F32).reshape(size, 2 * CH)
        out[pl.ds(at, size), :] = jnp.where((bins >= 0) & (bins < MAP), values, OUTSIDE)

    fill(fi, 8, ibuf[...], TILE_I * r - 8, PITCH)

    @pl.when(home == r)
    def _():
        fill(fj, 0, ibuf[pl.ds(4 * lax.rem(c, 2), 6)], TILE_J * c - 8, 48)

    @pl.when(home > r)
    def _():
        for k in range(5):
            arrived(jbuf, k, j_sem)

    @pl.when((home > r) & (c < COLS - 1))
    def _():
        arrived(jbuf, 5, j_sem)

    @pl.when(home < r)
    def _():
        pltpu.make_async_copy(jbuf, jbuf, block_sem.at[0]).wait()

    @pl.when(home != r)
    def _():
        fill(fj, 0, jbuf[...], TILE_J * c - 8, 48)

    for p in range(PAIR_J):
        for a in range(3):
            move = 2 * (a - 1)
            far = table[pl.ds(45 - p + move, PITCH), :]
            for tile in range(2):
                side = fi[pl.ds(8 + move, PITCH), pl.ds(tile * CH, CH)]
                value = side + fj[pl.ds(p + 2, 1), pl.ds((1 - tile) * CH, CH)] + far
                x1[tile, p, :, pl.ds(a * CH, CH)] = jnp.maximum(value, 0.0).astype(BF16)

    def first_conv(n, carry):
        q0 = 8 * n
        starts = (0, 1, 4, 5)
        for tile in range(2):
            lhs = jnp.concatenate(
                [jnp.concatenate([x1[tile, q0 + s + 2 * m] for m in range(4)], axis=1) for s in starts], axis=0
            )
            acc = jnp.dot(lhs, rhs1[tile].reshape(12 * CH, 2 * CH), preferred_element_type=F32)
            for k, s in enumerate(starts):
                for half in range(2):
                    q = q0 + s + 2 * half
                    j = TILE_J * c - 4 + q
                    scale = jnp.where((j >= 0) & (j < MAP), 1.0, 0.0)
                    conv = acc[PITCH * k : PITCH * (k + 1), CH * half : CH * (half + 1)]
                    base = x1[tile, q + 2, :, pl.ds(CH, CH)].astype(F32)
                    hidden = base + jnp.maximum(conv, 0.0) * (inside[...] * scale)
                    for a in range(3):
                        x2[tile, q, :, pl.ds(a * CH, CH)] = hidden[4 + 4 * a : 68 + 4 * a].astype(BF16)
        return carry

    lax.fori_loop(0, HID_J // 8, first_conv, 0)

    def second_conv(n, total):
        t0 = 8 * n
        accs = []
        for tile in range(2):
            lhs = jnp.concatenate(
                [jnp.concatenate([x2[tile, t0 + s + 4 * m] for m in range(4)], axis=1) for s in range(4)], axis=0
            )
            accs.append(jnp.dot(lhs, rhs2[tile].reshape(12 * CH, 2 * CH), preferred_element_type=F32))
        pieces = []
        for half in range(2):
            for s in range(4):
                hidden = 0.0
                for tile in range(2):
                    conv = accs[tile][TILE_I * s : TILE_I * (s + 1), CH * half : CH * (half + 1)]
                    base = x2[tile, t0 + s + 4 * half + 4, :, pl.ds(CH, CH)].astype(F32)
                    hidden = hidden + (base + jnp.maximum(conv, 0.0))
                high = hidden.astype(BF16)
                low = (hidden - high.astype(F32)).astype(BF16)
                pieces.append(jnp.concatenate([high, low], axis=1))
        points = jnp.dot(jnp.concatenate(pieces, axis=0), head, preferred_element_type=F32)
        for k in range(8):
            total = jnp.where(lane == t0 + k, points[TILE_I * k : TILE_I * (k + 1)], total)
        return total

    total = lax.fori_loop(0, TILE_J // 8, second_conv, jnp.zeros((TILE_I, CH), F32))
    out_ref[...] = 0.5 * total.T[:TILE_J]

    every_send(lambda copy: copy.wait_send())
    every_forward(lambda copy: copy.wait_send())


def on_device(embedding, bases_table, edit_pos, edit_tok, w_row, w_col, dist_gain, first_kernel, second_kernel, head_weight):
    channels = embedding.shape[1]
    operands = [
        embedding, bases_table, edit_pos.reshape(1, -1), edit_tok.reshape(1, -1), w_row, w_col,
        dist_gain.reshape(1, -1), first_kernel, second_kernel, head_weight.reshape(1, -1),
    ]
    turned = pl.pallas_call(
        kernel,
        out_shape=pltpu.VMEM((TILE_J, TILE_I), F32),
        in_specs=[pl.BlockSpec(memory_space=pltpu.HBM)] * 10,
        out_specs=pl.BlockSpec(memory_space=pltpu.VMEM),
        scratch_shapes=[
            pltpu.VMEM((32, channels), BF16),
            pltpu.VMEM((4, channels), BF16),
            pltpu.VMEM((1, 64), jnp.int32),
            pltpu.VMEM((1, 64), jnp.int32),
            pltpu.VMEM((channels, CH), BF16),
            pltpu.VMEM((channels, CH), BF16),
            pltpu.VMEM((1, CH), F32),
            pltpu.VMEM((1, CH), BF16),
            pltpu.VMEM((2, 4, 3, CH, 2 * CH), BF16),
            pltpu.VMEM((2, 4, 3, CH, 2 * CH), BF16),
            pltpu.VMEM((BINS, 2 * CH), BF16),
            pltpu.VMEM((10, BINS, 2 * CH), BF16),
            pltpu.VMEM((6, BINS, 2 * CH), BF16),
            pltpu.VMEM((96, 2 * CH), F32),
            pltpu.VMEM((48, 2 * CH), F32),
            pltpu.VMEM((128, CH), F32),
            pltpu.VMEM((PITCH, CH), F32),
            pltpu.VMEM((2, PAIR_J, PITCH, 3 * CH), BF16),
            pltpu.VMEM((2, HID_J, TILE_I, 3 * CH), BF16),
            pltpu.SemaphoreType.DMA((32,)),
            pltpu.SemaphoreType.DMA((24,)),
            pltpu.SemaphoreType.DMA((10,)),
            pltpu.SemaphoreType.DMA((6,)),
            pltpu.SemaphoreType.DMA((1,)),
        ],
        compiler_params=pltpu.CompilerParams(
            collective_id=0, has_side_effects=True, vmem_limit_bytes=48 * 1024 * 1024
        ),
    )(*[pltpu.with_memory_space_constraint(x, pltpu.HBM) for x in operands])
    return turned.T


def solution(mesh):
    placed = (P(("row", "col"), None), P(), P("cand"), P("cand"), P(), P(), P(), P(), P(), P())
    return jax.shard_map(
        on_device, mesh=mesh, in_specs=placed, out_specs=P(("cand", "row"), "col"), check_vma=False
    )
```

```python
import math

import jax
import jax.numpy as jnp
from jax import lax
from jax.experimental import pallas as pl
from jax.experimental.pallas import tpu as pltpu
from jax.sharding import PartitionSpec as P

MESH = pl.DeviceIdType.MESH
BF16 = jnp.bfloat16
F32 = jnp.float32

ROWS, COLS = 4, 8
BINS = 8
POOL = 4
CH = 128
TILE_I, TILE_J = 64, 32
MAP = 256
PITCH = 80
PAIR_J = 44
HID_J = 40
OUTSIDE = -1e30


def kernel(
    emb_h, tab_h, pos_h, tok_h, wr_h, wc_h, gain_h, k1_h, k2_h, hw_h,
    out_ref,
    emb, tab, pos, tok, wr, wc, gain, hw, rhs1, rhs2,
    proj, ibuf, jbuf, fi, fj, table, inside, x1, x2,
    in_sem, send_sem, i_sem, j_sem, block_sem, ready,
):
    r = lax.axis_index("row")
    c = lax.axis_index("col")
    g = r * COLS + c
    mine, part = g // 4, lax.rem(g, 4)
    left, right = mine - 1, mine + 1
    home = c // 2

    barrier = pltpu.get_barrier_semaphore()

    def tell(row, col):
        pl.semaphore_signal(barrier, inc=1, device_id={"row": row, "col": col}, device_id_type=MESH)

    @pl.when(r > 0)
    def _():
        tell(r - 1, COLS - 1)

    @pl.when(r < ROWS - 1)
    def _():
        tell(r + 1, 0)

    for k in range(1, COLS):
        tell(r, lax.rem(c + k, COLS))

    @pl.when(home > r)
    def _():
        for k in range(5):
            tell((4 * c - 1 + k) // COLS, lax.rem(4 * c - 1 + k, COLS))

    @pl.when((home > r) & (c < COLS - 1))
    def _():
        tell((4 * c + 4) // COLS, lax.rem(4 * c + 4, COLS))

    for row in range(1, ROWS):
        @pl.when((home == r) & (row > r))
        def _():
            tell(row, c)

    def load(src, dst, k):
        copy = pltpu.make_async_copy(src, dst, in_sem.at[k])
        copy.start()
        return copy

    first = [
        load(wr_h, wr, 0), load(wc_h, wc, 1), load(emb_h, emb, 2), load(tab_h, tab, 3), load(pos_h, pos, 4),
        load(tok_h, tok, 5),
    ]
    later = [load(gain_h, gain, 6), load(hw_h, hw, 7)]
    for n, (source, rhs) in enumerate(((k1_h, rhs1), (k2_h, rhs2))):
        for b in range(3):
            for tile, taps in ((0, source.at[:, b]), (1, source.at[b])):
                at = 8 + 12 * n + 4 * b + 2 * tile
                later.append(load(taps, rhs.at[tile, b, :, :, pl.ds(0, CH)], at))
                later.append(load(taps, rhs.at[tile, b + 1, :, :, pl.ds(CH, CH)], at + 1))

    for copy in first:
        copy.wait()
    own = lax.shift_right_logical(pos[...], 2) == g * BINS + lax.broadcasted_iota(jnp.int32, (BINS, 64), 0)
    token = jnp.broadcast_to(tok[...], (BINS, 64))
    pool = (
        lax.broadcasted_iota(jnp.int32, (BINS, 32), 1) // POOL == lax.broadcasted_iota(jnp.int32, (BINS, 32), 0)
    ).astype(BF16)
    total = jnp.dot(pool, emb[...], preferred_element_type=F32)
    bases = tab[...].astype(F32)
    for t in range(4):
        count = jnp.sum(jnp.where(own & (token == t), 1.0, 0.0), axis=1, keepdims=True)
        total = total + count * bases[t : t + 1, :]
    pooled = (total * (1.0 / POOL)).astype(BF16)
    proj[:, pl.ds(0, CH)] = jnp.dot(pooled, wr[...], preferred_element_type=F32).astype(BF16)
    proj[:, pl.ds(CH, CH)] = jnp.dot(pooled, wc[...], preferred_element_type=F32).astype(BF16)

    has_left = (part == 0) & (mine > 0)
    has_right = (part == 3) & (mine < COLS - 1)
    is_top = (c == 0) & (r > 0)
    is_bottom = (c == COLS - 1) & (r < ROWS - 1)
    pl.semaphore_wait(
        barrier,
        COLS - 1 + r
        + jnp.where(has_left, left // 2, 0) + jnp.where(has_right, right // 2, 0)
        + jnp.where(is_top | is_bottom, COLS, 0) + jnp.where(home < r, 1, 0),
    )

    def send(src, dst, k, rsem, row, col):
        return pltpu.make_async_remote_copy(
            src_ref=src, dst_ref=dst, send_sem=send_sem.at[k], recv_sem=rsem,
            device_id={"row": row, "col": col}, device_id_type=MESH,
        )

    def i_send(k, slot, row, col):
        return send(proj, ibuf.at[slot], k, i_sem.at[slot], row, col)

    def j_send(k, slot, row, col):
        return send(proj, jbuf.at[slot], k, j_sem.at[slot], row, col)

    def every_send(do):
        for row in range(ROWS - 1):
            @pl.when(row < r)
            def _():
                do(j_send(row, part + 1, row, mine))

        for row in range(ROWS - 1):
            @pl.when(has_left & (row < left // 2))
            def _():
                do(j_send(3 + row, 5, row, left))

        for row in range(ROWS - 1):
            @pl.when(has_right & (row < right // 2))
            def _():
                do(j_send(3 + row, 0, row, right))

        @pl.when(is_top)
        def _():
            for k in range(COLS):
                do(i_send(6 + k, 9, r - 1, k))

        @pl.when(is_bottom)
        def _():
            for k in range(COLS):
                do(i_send(6 + k, 0, r + 1, k))

        for k in range(1, COLS):
            do(i_send(13 + k, c + 1, r, lax.rem(c + k, COLS)))

    def every_forward(do):
        for row in range(1, ROWS):
            @pl.when((home == r) & (row > r))
            def _():
                block = ibuf.at[pl.ds(4 * lax.rem(c, 2), 6)]
                do(send(block, jbuf, 20 + row, block_sem.at[0], row, c))

    @pl.when(home < r)
    def _():
        pl.semaphore_signal(ready, inc=1, device_id={"row": home, "col": c}, device_id_type=MESH)

    every_send(lambda copy: copy.start())

    ibuf[c + 1] = proj[...]
    nothing = jnp.zeros((BINS, 2 * CH), BF16)

    @pl.when(r == 0)
    def _():
        ibuf[0] = nothing

    @pl.when(r == ROWS - 1)
    def _():
        ibuf[9] = nothing

    @pl.when((c == COLS - 1) & (home > r))
    def _():
        jbuf[5] = nothing

    blank = jnp.zeros((3, CH, CH), BF16)
    for rhs in (rhs1, rhs2):
        for tile in range(2):
            rhs[tile, 3, :, :, pl.ds(0, CH)] = blank
            rhs[tile, 0, :, :, pl.ds(CH, CH)] = blank
    for copy in later:
        copy.wait()
    offset = (TILE_I * r - TILE_J * c - 47 + lax.broadcasted_iota(jnp.int32, (128, CH), 0)).astype(F32)
    table[...] = gain[...] * (jnp.log(1.0 + jnp.abs(offset)) * (1.0 / math.log(MAP)))
    bin_i = TILE_I * r - 8 + lax.broadcasted_iota(jnp.int32, (PITCH, CH), 0)
    inside[...] = ((bin_i >= 0) & (bin_i < MAP)).astype(F32)
    fi[pl.ds(0, 8), :] = jnp.full((8, 2 * CH), OUTSIDE, F32)
    fi[pl.ds(88, 8), :] = jnp.full((8, 2 * CH), OUTSIDE, F32)
    head = jnp.concatenate([jnp.broadcast_to(hw[...].astype(F32), (CH, CH)).T.astype(BF16)] * 2, axis=0)
    lane = lax.broadcasted_iota(jnp.int32, (TILE_I, CH), 1)

    def arrived(buf, slot, sem):
        pltpu.make_async_copy(buf.at[slot], buf.at[slot], sem.at[slot]).wait()

    for k in range(1, COLS):
        arrived(ibuf, 1 + lax.rem(c + k, COLS), i_sem)

    @pl.when(r > 0)
    def _():
        arrived(ibuf, 0, i_sem)

    @pl.when(r < ROWS - 1)
    def _():
        arrived(ibuf, 9, i_sem)

    @pl.when((home == r) & (r < ROWS - 1))
    def _():
        pl.semaphore_wait(ready, ROWS - 1 - r)

    every_forward(lambda copy: copy.start())

    def fill(out, at, block, start, size):
        bins = start + lax.broadcasted_iota(jnp.int32, (size, 2 * CH), 0)
        values = block.astype(F32).reshape(size, 2 * CH)
        out[pl.ds(at, size), :] = jnp.where((bins >= 0) & (bins < MAP), values, OUTSIDE)

    fill(fi, 8, ibuf[...], TILE_I * r - 8, PITCH)

    @pl.when(home == r)
    def _():
        fill(fj, 0, ibuf[pl.ds(4 * lax.rem(c, 2), 6)], TILE_J * c - 8, 48)

    @pl.when(home > r)
    def _():
        for k in range(5):
            arrived(jbuf, k, j_sem)

    @pl.when((home > r) & (c < COLS - 1))
    def _():
        arrived(jbuf, 5, j_sem)

    @pl.when(home < r)
    def _():
        pltpu.make_async_copy(jbuf, jbuf, block_sem.at[0]).wait()

    @pl.when(home != r)
    def _():
        fill(fj, 0, jbuf[...], TILE_J * c - 8, 48)

    def pair_maps(first, end):
        for p in range(first, end):
            far = table[pl.ds(43 - p, PITCH + 4), :]
            for tile in range(2):
                side = fi[pl.ds(6, PITCH + 4), pl.ds(tile * CH, CH)]
                value = jnp.maximum(side + fj[pl.ds(p + 2, 1), pl.ds((1 - tile) * CH, CH)] + far, 0.0)
                for a in range(3):
                    x1[tile, p, :, pl.ds(a * CH, CH)] = value[2 * a : 2 * a + PITCH].astype(BF16)

    top, bottom = inside[pl.ds(0, 8), :], inside[pl.ds(PITCH - 8, 8), :]

    def first_conv(n):
        starts = [8 * n + s for s in (0, 1, 4, 5)]
        for tile in range(2):
            lhs = jnp.concatenate(
                [jnp.concatenate([x1[tile, q + 2 * m] for m in range(4)], axis=1) for q in starts], axis=0
            )
            acc = jnp.dot(lhs, rhs1[tile].reshape(12 * CH, 2 * CH), preferred_element_type=F32)
            for k in range(4):
                for half in range(2):
                    q = starts[k] + 2 * half
                    conv = jnp.maximum(acc[PITCH * k : PITCH * (k + 1), CH * half : CH * (half + 1)], 0.0)
                    conv = jnp.concatenate([conv[:8] * top, conv[8 : PITCH - 8], conv[PITCH - 8 :] * bottom], axis=0)
                    if q < 4:
                        conv = conv * jnp.where(c > 0, 1.0, 0.0)
                    if q >= HID_J - 4:
                        conv = conv * jnp.where(c < COLS - 1, 1.0, 0.0)
                    hidden = x1[tile, q + 2, :, pl.ds(CH, CH)].astype(F32) + conv
                    for a in range(3):
                        x2[tile, q, :, pl.ds(a * CH, CH)] = hidden[4 + 4 * a : 68 + 4 * a].astype(BF16)

    def second_conv(n, total):
        t0 = 8 * n
        accs = []
        for tile in range(2):
            lhs = jnp.concatenate(
                [jnp.concatenate([x2[tile, t0 + s + 4 * m] for m in range(4)], axis=1) for s in range(4)], axis=0
            )
            accs.append(jnp.dot(lhs, rhs2[tile].reshape(12 * CH, 2 * CH), preferred_element_type=F32))
        pieces = []
        for half in range(2):
            for s in range(4):
                hidden = 0.0
                for tile in range(2):
                    conv = accs[tile][TILE_I * s : TILE_I * (s + 1), CH * half : CH * (half + 1)]
                    base = x2[tile, t0 + s + 4 * half + 4, :, pl.ds(CH, CH)].astype(F32)
                    hidden = hidden + (base + jnp.maximum(conv, 0.0))
                high = hidden.astype(BF16)
                low = (hidden - high.astype(F32)).astype(BF16)
                pieces.append(jnp.concatenate([high, low], axis=1))
        points = jnp.dot(jnp.concatenate(pieces, axis=0), head, preferred_element_type=F32)
        for k in range(8):
            total = jnp.where(lane == t0 + k, points[TILE_I * k : TILE_I * (k + 1)], total)
        return total

    total = jnp.zeros((TILE_I, CH), F32)
    pair_maps(0, 12)
    for n in range(HID_J // 8):
        pair_maps(8 * n + 12, min(8 * n + 20, PAIR_J))
        first_conv(n)
        if n > 0:
            total = second_conv(n - 1, total)
    out_ref[...] = 0.5 * total.T[:TILE_J]

    every_send(lambda copy: copy.wait_send())
    every_forward(lambda copy: copy.wait_send())


def on_device(embedding, bases_table, edit_pos, edit_tok, w_row, w_col, dist_gain, first_kernel, second_kernel, head_weight):
    channels = embedding.shape[1]
    operands = [
        embedding, bases_table, edit_pos.reshape(1, -1), edit_tok.reshape(1, -1), w_row, w_col,
        dist_gain.reshape(1, -1), first_kernel, second_kernel, head_weight.reshape(1, -1),
    ]
    turned = pl.pallas_call(
        kernel,
        out_shape=pltpu.VMEM((TILE_J, TILE_I), F32),
        in_specs=[pl.BlockSpec(memory_space=pltpu.HBM)] * 10,
        out_specs=pl.BlockSpec(memory_space=pltpu.VMEM),
        scratch_shapes=[
            pltpu.VMEM((32, channels), BF16),
            pltpu.VMEM((4, channels), BF16),
            pltpu.VMEM((1, 64), jnp.int32),
            pltpu.VMEM((1, 64), jnp.int32),
            pltpu.VMEM((channels, CH), BF16),
            pltpu.VMEM((channels, CH), BF16),
            pltpu.VMEM((1, CH), F32),
            pltpu.VMEM((1, CH), BF16),
            pltpu.VMEM((2, 4, 3, CH, 2 * CH), BF16),
            pltpu.VMEM((2, 4, 3, CH, 2 * CH), BF16),
            pltpu.VMEM((BINS, 2 * CH), BF16),
            pltpu.VMEM((10, BINS, 2 * CH), BF16),
            pltpu.VMEM((6, BINS, 2 * CH), BF16),
            pltpu.VMEM((96, 2 * CH), F32),
            pltpu.VMEM((48, 2 * CH), F32),
            pltpu.VMEM((128, CH), F32),
            pltpu.VMEM((PITCH, CH), F32),
            pltpu.VMEM((2, PAIR_J, PITCH, 3 * CH), BF16),
            pltpu.VMEM((2, HID_J, TILE_I, 3 * CH), BF16),
            pltpu.SemaphoreType.DMA((32,)),
            pltpu.SemaphoreType.DMA((24,)),
            pltpu.SemaphoreType.DMA((10,)),
            pltpu.SemaphoreType.DMA((6,)),
            pltpu.SemaphoreType.DMA((1,)),
            pltpu.SemaphoreType.REGULAR,
        ],
        compiler_params=pltpu.CompilerParams(
            collective_id=0, has_side_effects=True, vmem_limit_bytes=48 * 1024 * 1024
        ),
    )(*[pltpu.with_memory_space_constraint(x, pltpu.HBM) for x in operands])
    return turned.T


def solution(mesh):
    placed = (P(("row", "col"), None), P(), P("cand"), P("cand"), P(), P(), P(), P(), P(), P())
    return jax.shard_map(
        on_device, mesh=mesh, in_specs=placed, out_specs=P(("cand", "row"), "col"), check_vma=False
    )
```

```python
import math

import jax
import jax.numpy as jnp
from jax import lax
from jax.experimental import pallas as pl
from jax.experimental.pallas import tpu as pltpu
from jax.sharding import PartitionSpec as P

MESH = pl.DeviceIdType.MESH
BF16 = jnp.bfloat16
F32 = jnp.float32

ROWS, COLS = 4, 8
BINS = 8
POOL = 4
CH = 128
TILE_I, TILE_J = 64, 32
MAP = 256
LONG = 80
PITCH = 72
PAIR_J = 44
HID_J = 40
OUTSIDE = -1e30


def kernel(
    emb_h, tab_h, pos_h, tok_h, wr_h, wc_h, gain_h, k1_h, k2_h, hw_h,
    out_ref,
    emb, tab, pos, tok, w, gain, hw, rhs1, rhs2,
    proj, ibuf, jbuf, fi, fj, table, inside, x1, x2,
    in_sem, send_sem, i_sem, j_sem, block_sem, ready,
):
    r = lax.axis_index("row")
    c = lax.axis_index("col")
    g = r * COLS + c
    mine, part = g // 4, lax.rem(g, 4)
    left, right = mine - 1, mine + 1
    home = c // 2

    barrier = pltpu.get_barrier_semaphore()

    def tell(row, col):
        pl.semaphore_signal(barrier, inc=1, device_id={"row": row, "col": col}, device_id_type=MESH)

    for k in range(1, COLS):
        tell(r, lax.rem(c + k, COLS))

    def load(src, dst, k):
        copy = pltpu.make_async_copy(src, dst, in_sem.at[k])
        copy.start()
        return copy

    first = [load(emb_h, emb, 2), load(tab_h, tab, 3), load(pos_h, pos, 4), load(tok_h, tok, 5)]
    weights = [load(wr_h, w.at[:, pl.ds(0, CH)], 0), load(wc_h, w.at[:, pl.ds(CH, CH)], 1)]

    @pl.when(r > 0)
    def _():
        tell(r - 1, COLS - 1)

    @pl.when(r < ROWS - 1)
    def _():
        tell(r + 1, 0)

    @pl.when(home > r)
    def _():
        for k in range(5):
            tell((4 * c - 1 + k) // COLS, lax.rem(4 * c - 1 + k, COLS))

    @pl.when((home > r) & (c < COLS - 1))
    def _():
        tell((4 * c + 4) // COLS, lax.rem(4 * c + 4, COLS))

    for row in range(1, ROWS):
        @pl.when((home == r) & (row > r) & ((home > 0) | (row != 2)))
        def _():
            tell(row, c)

    @pl.when((home == 0) & (r == 1))
    def _():
        tell(2, c)

    for copy in first:
        copy.wait()
    own = lax.shift_right_logical(pos[...], 2) == g * BINS + lax.broadcasted_iota(jnp.int32, (BINS, 64), 0)
    token = jnp.broadcast_to(tok[...], (BINS, 64))
    pool = (
        lax.broadcasted_iota(jnp.int32, (BINS, 32), 1) // POOL == lax.broadcasted_iota(jnp.int32, (BINS, 32), 0)
    ).astype(BF16)
    total = jnp.dot(pool, emb[...], preferred_element_type=F32)
    bases = tab[...].astype(F32)
    for t in range(4):
        count = jnp.sum(jnp.where(own & (token == t), 1.0, 0.0), axis=1, keepdims=True)
        total = total + count * bases[t : t + 1, :]
    pooled = (total * (1.0 / POOL)).astype(BF16)
    for copy in weights:
        copy.wait()
    proj[...] = jnp.dot(pooled, w[...], preferred_element_type=F32).astype(BF16)

    has_left = (part == 0) & (mine > 0)
    has_right = (part == 3) & (mine < COLS - 1)
    is_top = (c == 0) & (r > 0)
    is_bottom = (c == COLS - 1) & (r < ROWS - 1)
    pl.semaphore_wait(
        barrier,
        COLS - 1 + r
        + jnp.where(has_left, left // 2, 0) + jnp.where(has_right, right // 2, 0)
        + jnp.where(is_top | is_bottom, COLS, 0) + jnp.where(home < r, 1, 0),
    )

    def send(src, dst, k, rsem, row, col):
        return pltpu.make_async_remote_copy(
            src_ref=src, dst_ref=dst, send_sem=send_sem.at[k], recv_sem=rsem,
            device_id={"row": row, "col": col}, device_id_type=MESH,
        )

    def j_send(k, slot, row, col):
        return send(proj, jbuf.at[slot], k, j_sem.at[0], row, col)

    def i_send(k, slot, row, col):
        send(proj, ibuf.at[slot], k, i_sem.at[0], row, col).start()

    def every_j_send(do):
        for row in range(ROWS - 1):
            @pl.when(row < r)
            def _():
                do(j_send(2 + row, part + 1, row, mine))

        for row in range(ROWS - 1):
            @pl.when(has_left & (row < left // 2))
            def _():
                do(j_send(5 + row, 5, row, left))

        for row in range(ROWS - 1):
            @pl.when(has_right & (row < right // 2))
            def _():
                do(j_send(5 + row, 0, row, right))

    def every_i_send():
        @pl.when(is_top)
        def _():
            for k in range(COLS):
                i_send(1, 9, r - 1, k)

        @pl.when(is_bottom)
        def _():
            for k in range(COLS):
                i_send(1, 0, r + 1, k)

        for k in range(1, COLS):
            i_send(0, c + 1, r, lax.rem(c + k, COLS))

    block = ibuf.at[pl.ds(4 * lax.rem(c, 2), 6)]
    source = jnp.where((home == 0) & (r == 2), 1, home)

    def forward(src, row):
        return send(src, jbuf, 8 + row, block_sem.at[0], row, c)

    def every_forward(do):
        for row in (1, 3, 2):
            @pl.when((home == r) & (row > r) & ((home > 0) | (row != 2)))
            def _():
                do(forward(block, row), row)

    relays = (home == 0) & (r == 1)

    every_j_send(lambda copy: copy.start())
    @pl.when(home < r)
    def _():
        pl.semaphore_signal(ready.at[r], inc=1, device_id={"row": source, "col": c}, device_id_type=MESH)

    every_i_send()


    later = [load(gain_h, gain, 6), load(hw_h, hw, 7)]
    for n, (source, rhs) in enumerate(((k1_h, rhs1), (k2_h, rhs2))):
        for b in range(3):
            for tile, taps in ((0, source.at[:, b]), (1, source.at[b])):
                at = 8 + 12 * n + 4 * b + 2 * tile
                later.append(load(taps, rhs.at[tile, b, :, :, pl.ds(0, CH)], at))
                later.append(load(taps, rhs.at[tile, b + 1, :, :, pl.ds(CH, CH)], at + 1))

    ibuf[c + 1] = proj[...]
    nothing = jnp.zeros((BINS, 2 * CH), BF16)

    @pl.when(r == 0)
    def _():
        ibuf[0] = nothing

    @pl.when(r == ROWS - 1)
    def _():
        ibuf[9] = nothing

    @pl.when((c == COLS - 1) & (home > r))
    def _():
        jbuf[5] = nothing

    blank = jnp.zeros((3, CH, CH), BF16)
    for rhs in (rhs1, rhs2):
        for tile in range(2):
            rhs[tile, 3, :, :, pl.ds(0, CH)] = blank
            rhs[tile, 0, :, :, pl.ds(CH, CH)] = blank
    for copy in later:
        copy.wait()
    offset = (TILE_I * r - TILE_J * c - 43 + lax.broadcasted_iota(jnp.int32, (128, CH), 0)).astype(F32)
    table[...] = gain[...] * (jnp.log(1.0 + jnp.abs(offset)) * (1.0 / math.log(MAP)))
    bin_i = TILE_I * r - 4 + lax.broadcasted_iota(jnp.int32, (PITCH, CH), 0)
    inside[...] = ((bin_i >= 0) & (bin_i < MAP)).astype(F32)
    head = jnp.broadcast_to(hw[...].astype(F32), (CH, CH)).T.astype(BF16)
    lane = lax.broadcasted_iota(jnp.int32, (TILE_I, CH), 1)

    def arrived(buf, count, sem):
        some = buf.at[pl.ds(0, count)]
        pltpu.make_async_copy(some, some, sem.at[0]).wait()

    inner = (r > 0) & (r < ROWS - 1)

    @pl.when(inner)
    def _():
        arrived(ibuf, COLS + 1, i_sem)

    @pl.when(jnp.logical_not(inner))
    def _():
        arrived(ibuf, COLS, i_sem)

    def forward_now(copy, row):
        pl.semaphore_wait(ready.at[row], 1)
        copy.start()

    every_forward(forward_now)

    def fill(out, at, block, start, size):
        bins = start + lax.broadcasted_iota(jnp.int32, (size, 2 * CH), 0)
        values = block.astype(F32).reshape(size, 2 * CH)
        out[pl.ds(at, size), :] = jnp.where((bins >= 0) & (bins < MAP), values, OUTSIDE)

    fill(fi, 0, ibuf[...], TILE_I * r - 8, LONG)

    @pl.when(home == r)
    def _():
        fill(fj, 0, ibuf[pl.ds(4 * lax.rem(c, 2), 6)], TILE_J * c - 8, 48)

    @pl.when((home > r) & (c < COLS - 1))
    def _():
        arrived(jbuf, 6, j_sem)

    @pl.when((home > r) & (c == COLS - 1))
    def _():
        arrived(jbuf, 5, j_sem)

    @pl.when(home < r)
    def _():
        arrived(jbuf, 6, block_sem)

    @pl.when(relays)
    def _():
        forward_now(forward(jbuf, 2), 2)

    @pl.when(home != r)
    def _():
        fill(fj, 0, jbuf[...], TILE_J * c - 8, 48)

    def pair_maps(first, end):
        for p in range(first, end):
            far = table[pl.ds(43 - p, PITCH + 4), :]
            for tile in range(2):
                side = fi[pl.ds(2, PITCH + 4), pl.ds(tile * CH, CH)]
                value = jnp.maximum(side + fj[pl.ds(p + 2, 1), pl.ds((1 - tile) * CH, CH)] + far, 0.0)
                for a in range(3):
                    x1[tile, p, :, pl.ds(a * CH, CH)] = value[2 * a : 2 * a + PITCH].astype(BF16)

    top, bottom = inside[pl.ds(0, 8), :], inside[pl.ds(PITCH - 8, 8), :]

    def first_conv(n):
        starts = [8 * n + s for s in (0, 1, 4, 5)]
        for tile in range(2):
            lhs = jnp.concatenate(
                [jnp.concatenate([x1[tile, q + 2 * m] for m in range(4)], axis=1) for q in starts], axis=0
            )
            acc = jnp.dot(lhs, rhs1[tile].reshape(12 * CH, 2 * CH), preferred_element_type=F32)
            for k in range(4):
                for half in range(2):
                    q = starts[k] + 2 * half
                    conv = jnp.maximum(acc[PITCH * k : PITCH * (k + 1), CH * half : CH * (half + 1)], 0.0)
                    conv = jnp.concatenate([conv[:8] * top, conv[8 : PITCH - 8], conv[PITCH - 8 :] * bottom], axis=0)
                    if q < 4:
                        conv = conv * jnp.where(c > 0, 1.0, 0.0)
                    if q >= HID_J - 4:
                        conv = conv * jnp.where(c < COLS - 1, 1.0, 0.0)
                    hidden = x1[tile, q + 2, :, pl.ds(CH, CH)].astype(F32) + conv
                    for a in range(3):
                        x2[tile, q, :, pl.ds(a * CH, CH)] = hidden[4 * a : TILE_I + 4 * a].astype(BF16)

    def second_conv(n, total):
        t0 = 8 * n
        accs = []
        for tile in range(2):
            lhs = jnp.concatenate(
                [jnp.concatenate([x2[tile, t0 + s + 4 * m] for m in range(4)], axis=1) for s in range(4)], axis=0
            )
            accs.append(jnp.dot(lhs, rhs2[tile].reshape(12 * CH, 2 * CH), preferred_element_type=F32))
        pieces = []
        for half in range(2):
            for s in range(4):
                hidden = 0.0
                for tile in range(2):
                    conv = accs[tile][TILE_I * s : TILE_I * (s + 1), CH * half : CH * (half + 1)]
                    base = x2[tile, t0 + s + 4 * half + 4, :, pl.ds(CH, CH)].astype(F32)
                    hidden = hidden + (base + jnp.maximum(conv, 0.0))
                pieces.append(hidden.astype(BF16))
        points = jnp.dot(jnp.concatenate(pieces, axis=0), head, preferred_element_type=F32)
        for k in range(8):
            total = jnp.where(lane == t0 + k, points[TILE_I * k : TILE_I * (k + 1)], total)
        return total

    total = jnp.zeros((TILE_I, CH), F32)
    pair_maps(0, 12)
    for n in range(HID_J // 8):
        pair_maps(8 * n + 12, min(8 * n + 20, PAIR_J))
        first_conv(n)
        if n > 0:
            total = second_conv(n - 1, total)
    out_ref[...] = 0.5 * total.T[:TILE_J]

    def sent(count, k):
        some = ibuf.at[pl.ds(0, count)]
        pltpu.make_async_copy(some, some, send_sem.at[k]).wait()

    sent(COLS - 1, 0)

    @pl.when(is_top | is_bottom)
    def _():
        sent(COLS, 1)

    every_j_send(lambda copy: copy.wait_send())
    every_forward(lambda copy, row: copy.wait_send())

    @pl.when(relays)
    def _():
        forward(jbuf, 2).wait_send()


def on_device(embedding, bases_table, edit_pos, edit_tok, w_row, w_col, dist_gain, first_kernel, second_kernel, head_weight):
    channels = embedding.shape[1]
    operands = [
        embedding, bases_table, edit_pos.reshape(1, -1), edit_tok.reshape(1, -1), w_row, w_col,
        dist_gain.reshape(1, -1), first_kernel, second_kernel, head_weight.reshape(1, -1),
    ]
    turned = pl.pallas_call(
        kernel,
        out_shape=pltpu.VMEM((TILE_J, TILE_I), F32),
        in_specs=[pl.BlockSpec(memory_space=pltpu.HBM)] * 10,
        out_specs=pl.BlockSpec(memory_space=pltpu.VMEM),
        scratch_shapes=[
            pltpu.VMEM((32, channels), BF16),
            pltpu.VMEM((4, channels), BF16),
            pltpu.VMEM((1, 64), jnp.int32),
            pltpu.VMEM((1, 64), jnp.int32),
            pltpu.VMEM((channels, 2 * CH), BF16),
            pltpu.VMEM((1, CH), F32),
            pltpu.VMEM((1, CH), BF16),
            pltpu.VMEM((2, 4, 3, CH, 2 * CH), BF16),
            pltpu.VMEM((2, 4, 3, CH, 2 * CH), BF16),
            pltpu.VMEM((BINS, 2 * CH), BF16),
            pltpu.VMEM((10, BINS, 2 * CH), BF16),
            pltpu.VMEM((6, BINS, 2 * CH), BF16),
            pltpu.VMEM((LONG, 2 * CH), F32),
            pltpu.VMEM((48, 2 * CH), F32),
            pltpu.VMEM((128, CH), F32),
            pltpu.VMEM((PITCH, CH), F32),
            pltpu.VMEM((2, PAIR_J, PITCH, 3 * CH), BF16),
            pltpu.VMEM((2, HID_J, TILE_I, 3 * CH), BF16),
            pltpu.SemaphoreType.DMA((32,)),
            pltpu.SemaphoreType.DMA((12,)),
            pltpu.SemaphoreType.DMA((1,)),
            pltpu.SemaphoreType.DMA((1,)),
            pltpu.SemaphoreType.DMA((1,)),
            pltpu.SemaphoreType.REGULAR((ROWS,)),
        ],
        compiler_params=pltpu.CompilerParams(
            collective_id=0, has_side_effects=True, vmem_limit_bytes=48 * 1024 * 1024
        ),
    )(*[pltpu.with_memory_space_constraint(x, pltpu.HBM) for x in operands])
    return turned.T


def solution(mesh):
    placed = (P(("row", "col"), None), P(), P("cand"), P("cand"), P(), P(), P(), P(), P(), P())
    return jax.shard_map(
        on_device, mesh=mesh, in_specs=placed, out_specs=P(("cand", "row"), "col"), check_vma=False
    )
```

```python
import math

import jax
import jax.numpy as jnp
from jax import lax
from jax.experimental import pallas as pl
from jax.experimental.pallas import tpu as pltpu
from jax.sharding import PartitionSpec as P

MESH = pl.DeviceIdType.MESH
BF16 = jnp.bfloat16
F32 = jnp.float32

ROWS, COLS = 4, 8
BINS = 8
POOL = 4
CH = 128
TILE_I, TILE_J = 64, 32
MAP = 256
LONG = 80
PITCH = 72
PAIR_J = 44
HID_J = 40
OUTSIDE = -1e30


def kernel(
    emb_h, tab_h, pos_h, tok_h, wr_h, wc_h, gain_h, k1_h, k2_h, hw_h,
    out_ref,
    emb, tab, pos, tok, w, gain, hw, rhs1, rhs2,
    proj, ibuf, jbuf, fi, fj, table, inside, x1a, x1b, x1c, x2a, x2b, x2c, moved, kept,
    in_sem, send_sem, i_sem, j_sem, block_sem, ready,
):
    r = lax.axis_index("row")
    c = lax.axis_index("col")
    g = r * COLS + c
    mine, part = g // 4, lax.rem(g, 4)
    left, right = mine - 1, mine + 1
    home = c // 2

    barrier = pltpu.get_barrier_semaphore()

    def tell(row, col):
        pl.semaphore_signal(barrier, inc=1, device_id={"row": row, "col": col}, device_id_type=MESH)

    for k in range(1, COLS):
        tell(r, lax.rem(c + k, COLS))

    def load(src, dst, k):
        copy = pltpu.make_async_copy(src, dst, in_sem.at[k])
        copy.start()
        return copy

    first = [load(emb_h, emb, 2), load(tab_h, tab, 3), load(pos_h, pos, 4), load(tok_h, tok, 5)]
    weights = [load(wr_h, w.at[:, pl.ds(0, CH)], 0), load(wc_h, w.at[:, pl.ds(CH, CH)], 1)]

    @pl.when(r > 0)
    def _():
        tell(r - 1, COLS - 1)

    @pl.when(r < ROWS - 1)
    def _():
        tell(r + 1, 0)

    @pl.when(home > r)
    def _():
        for k in range(5):
            tell((4 * c - 1 + k) // COLS, lax.rem(4 * c - 1 + k, COLS))

    @pl.when((home > r) & (c < COLS - 1))
    def _():
        tell((4 * c + 4) // COLS, lax.rem(4 * c + 4, COLS))

    for row in range(1, ROWS):
        @pl.when((home == r) & (row > r) & ((home > 0) | (row != 2)))
        def _():
            tell(row, c)

    @pl.when((home == 0) & (r == 1))
    def _():
        tell(2, c)

    for copy in first:
        copy.wait()
    own = lax.shift_right_logical(pos[...], 2) == g * BINS + lax.broadcasted_iota(jnp.int32, (BINS, 64), 0)
    token = jnp.broadcast_to(tok[...], (BINS, 64))
    pool = (
        lax.broadcasted_iota(jnp.int32, (BINS, 32), 1) // POOL == lax.broadcasted_iota(jnp.int32, (BINS, 32), 0)
    ).astype(BF16)
    total = jnp.dot(pool, emb[...], preferred_element_type=F32)
    bases = tab[...].astype(F32)
    for t in range(4):
        count = jnp.sum(jnp.where(own & (token == t), 1.0, 0.0), axis=1, keepdims=True)
        total = total + count * bases[t : t + 1, :]
    pooled = (total * (1.0 / POOL)).astype(BF16)
    for copy in weights:
        copy.wait()
    proj[...] = jnp.dot(pooled, w[...], preferred_element_type=F32).astype(BF16)

    has_left = (part == 0) & (mine > 0)
    has_right = (part == 3) & (mine < COLS - 1)
    is_top = (c == 0) & (r > 0)
    is_bottom = (c == COLS - 1) & (r < ROWS - 1)
    pl.semaphore_wait(
        barrier,
        COLS - 1 + r
        + jnp.where(has_left, left // 2, 0) + jnp.where(has_right, right // 2, 0)
        + jnp.where(is_top | is_bottom, COLS, 0) + jnp.where(home < r, 1, 0),
    )

    def send(src, dst, k, rsem, row, col):
        return pltpu.make_async_remote_copy(
            src_ref=src, dst_ref=dst, send_sem=send_sem.at[k], recv_sem=rsem,
            device_id={"row": row, "col": col}, device_id_type=MESH,
        )

    def j_send(k, slot, row, col):
        return send(proj, jbuf.at[slot], k, j_sem.at[0], row, col)

    def i_send(k, slot, row, col):
        send(proj, ibuf.at[slot], k, i_sem.at[0], row, col).start()

    def every_j_send(do):
        for row in range(ROWS - 1):
            @pl.when(has_left & (row < left // 2))
            def _():
                do(j_send(5 + row, 5, row, left))

        for row in range(ROWS - 1):
            @pl.when(has_right & (row < right // 2))
            def _():
                do(j_send(5 + row, 0, row, right))

        for row in range(ROWS - 1):
            @pl.when(row < r)
            def _():
                do(j_send(2 + row, part + 1, row, mine))

    def every_i_send():
        @pl.when(is_top)
        def _():
            for k in range(COLS):
                i_send(1, 9, r - 1, k)

        @pl.when(is_bottom)
        def _():
            for k in range(COLS):
                i_send(1, 0, r + 1, k)

        for k in range(1, COLS):
            i_send(0, c + 1, r, lax.rem(c + k, COLS))

    block = ibuf.at[pl.ds(4 * lax.rem(c, 2), 6)]
    source = jnp.where((home == 0) & (r == 2), 1, home)

    def forward(src, row):
        return send(src, jbuf, 8 + row, block_sem.at[0], row, c)

    def every_forward(do):
        for row in (1, 3, 2):
            @pl.when((home == r) & (row > r) & ((home > 0) | (row != 2)))
            def _():
                do(forward(block, row), row)

    relays = (home == 0) & (r == 1)

    every_j_send(lambda copy: copy.start())
    @pl.when(home < r)
    def _():
        pl.semaphore_signal(ready.at[r], inc=1, device_id={"row": source, "col": c}, device_id_type=MESH)

    every_i_send()


    later = [load(gain_h, gain, 6), load(hw_h, hw, 7)]
    for n, (source, rhs) in enumerate(((k1_h, rhs1), (k2_h, rhs2))):
        for b in range(3):
            for tile, taps in ((0, source.at[:, b]), (1, source.at[b])):
                at = 8 + 12 * n + 4 * b + 2 * tile
                later.append(load(taps, rhs.at[tile, b, :, :, pl.ds(0, CH)], at))
                later.append(load(taps, rhs.at[tile, b + 1, :, :, pl.ds(CH, CH)], at + 1))

    ibuf[c + 1] = proj[...]
    nothing = jnp.zeros((BINS, 2 * CH), BF16)

    @pl.when(r == 0)
    def _():
        ibuf[0] = nothing

    @pl.when(r == ROWS - 1)
    def _():
        ibuf[9] = nothing

    @pl.when((c == COLS - 1) & (home > r))
    def _():
        jbuf[5] = nothing

    blank = jnp.zeros((3, CH, CH), BF16)
    for rhs in (rhs1, rhs2):
        for tile in range(2):
            rhs[tile, 3, :, :, pl.ds(0, CH)] = blank
            rhs[tile, 0, :, :, pl.ds(CH, CH)] = blank
    for copy in later:
        copy.wait()
    offset = (TILE_I * r - TILE_J * c - 43 + lax.broadcasted_iota(jnp.int32, (128, CH), 0)).astype(F32)
    table[...] = gain[...] * (jnp.log(1.0 + jnp.abs(offset)) * (1.0 / math.log(MAP)))
    bin_i = TILE_I * r - 4 + lax.broadcasted_iota(jnp.int32, (PITCH, CH), 0)
    inside[...] = ((bin_i >= 0) & (bin_i < MAP)).astype(F32)
    head = jnp.broadcast_to(hw[...].astype(F32), (CH, CH)).T.astype(BF16)
    lane = lax.broadcasted_iota(jnp.int32, (TILE_I, CH), 1)

    def arrived(buf, count, sem):
        some = buf.at[pl.ds(0, count)]
        pltpu.make_async_copy(some, some, sem.at[0]).wait()

    inner = (r > 0) & (r < ROWS - 1)

    @pl.when(inner)
    def _():
        arrived(ibuf, COLS + 1, i_sem)

    @pl.when(jnp.logical_not(inner))
    def _():
        arrived(ibuf, COLS, i_sem)

    def forward_now(copy, row):
        pl.semaphore_wait(ready.at[row], 1)
        copy.start()

    every_forward(forward_now)

    def fill(out, at, block, start, size):
        bins = start + lax.broadcasted_iota(jnp.int32, (size, 2 * CH), 0)
        values = block.astype(F32).reshape(size, 2 * CH)
        out[pl.ds(at, size), :] = jnp.where((bins >= 0) & (bins < MAP), values, OUTSIDE)

    fill(fi, 0, ibuf[...], TILE_I * r - 8, LONG)

    @pl.when(home == r)
    def _():
        fill(fj, 0, ibuf[pl.ds(4 * lax.rem(c, 2), 6)], TILE_J * c - 8, 48)

    @pl.when((home > r) & (c < COLS - 1))
    def _():
        arrived(jbuf, 6, j_sem)

    @pl.when((home > r) & (c == COLS - 1))
    def _():
        arrived(jbuf, 5, j_sem)

    @pl.when(home < r)
    def _():
        arrived(jbuf, 6, block_sem)

    @pl.when(relays)
    def _():
        forward_now(forward(jbuf, 2), 2)

    @pl.when(home != r)
    def _():
        fill(fj, 0, jbuf[...], TILE_J * c - 8, 48)

    x1, x2 = (x1a, x1b, x1c), (x2a, x2b, x2c)

    def pair_maps(first, end):
        for p in range(first, end):
            far = table[pl.ds(43 - p, PITCH + 4), :]
            for tile in range(2):
                side = fi[pl.ds(2, PITCH + 4), pl.ds(tile * CH, CH)]
                value = jnp.maximum(side + fj[pl.ds(p + 2, 1), pl.ds((1 - tile) * CH, CH)] + far, 0.0)
                slot = (2 * p + tile) % 8
                moved[slot, pl.ds(0, PITCH + 4), :] = value
                x1[0][tile, p] = value[:PITCH].astype(BF16)
                for a in (1, 2):
                    x1[a][tile, p] = moved[slot, pl.ds(2 * a, PITCH), :].astype(BF16)

    top, bottom = inside[pl.ds(0, 8), :], inside[pl.ds(PITCH - 8, 8), :]

    def first_conv(n):
        starts = [8 * n + s for s in (0, 1, 4, 5)]
        for tile in range(2):
            lhs = jnp.concatenate(
                [jnp.concatenate([x1[a][tile, q + 2 * m] for m in range(4) for a in range(3)], axis=1) for q in starts], axis=0
            )
            acc = jnp.dot(lhs, rhs1[tile].reshape(12 * CH, 2 * CH), preferred_element_type=F32)
            for k in range(4):
                for half in range(2):
                    q = starts[k] + 2 * half
                    conv = jnp.maximum(acc[PITCH * k : PITCH * (k + 1), CH * half : CH * (half + 1)], 0.0)
                    conv = jnp.concatenate([conv[:8] * top, conv[8 : PITCH - 8], conv[PITCH - 8 :] * bottom], axis=0)
                    if q < 4:
                        conv = conv * jnp.where(c > 0, 1.0, 0.0)
                    if q >= HID_J - 4:
                        conv = conv * jnp.where(c < COLS - 1, 1.0, 0.0)
                    hidden = x1[1][tile, q + 2].astype(F32) + conv
                    kept[q % 8] = hidden
                    x2[0][tile, q] = hidden[:TILE_I].astype(BF16)
                    x2[1][tile, q] = kept[q % 8, pl.ds(4, TILE_I), :].astype(BF16)
                    x2[2][tile, q] = hidden[8:].astype(BF16)

    def second_conv(n, total):
        t0 = 8 * n
        accs = []
        for tile in range(2):
            lhs = jnp.concatenate(
                [jnp.concatenate([x2[a][tile, t0 + s + 4 * m] for m in range(4) for a in range(3)], axis=1) for s in range(4)], axis=0
            )
            accs.append(jnp.dot(lhs, rhs2[tile].reshape(12 * CH, 2 * CH), preferred_element_type=F32))
        pieces = []
        for half in range(2):
            for s in range(4):
                hidden = 0.0
                for tile in range(2):
                    conv = accs[tile][TILE_I * s : TILE_I * (s + 1), CH * half : CH * (half + 1)]
                    base = x2[1][tile, t0 + s + 4 * half + 4].astype(F32)
                    hidden = hidden + (base + jnp.maximum(conv, 0.0))
                pieces.append(hidden.astype(BF16))
        points = jnp.dot(jnp.concatenate(pieces, axis=0), head, preferred_element_type=F32)
        for k in range(8):
            total = jnp.where(lane == t0 + k, points[TILE_I * k : TILE_I * (k + 1)], total)
        return total

    total = jnp.zeros((TILE_I, CH), F32)
    pair_maps(0, 12)
    for n in range(HID_J // 8):
        pair_maps(8 * n + 12, min(8 * n + 20, PAIR_J))
        first_conv(n)
        if n > 0:
            total = second_conv(n - 1, total)
    out_ref[...] = 0.5 * total.T[:TILE_J]

    def sent(count, k):
        some = ibuf.at[pl.ds(0, count)]
        pltpu.make_async_copy(some, some, send_sem.at[k]).wait()

    sent(COLS - 1, 0)

    @pl.when(is_top | is_bottom)
    def _():
        sent(COLS, 1)

    every_j_send(lambda copy: copy.wait_send())
    every_forward(lambda copy, row: copy.wait_send())

    @pl.when(relays)
    def _():
        forward(jbuf, 2).wait_send()


def on_device(embedding, bases_table, edit_pos, edit_tok, w_row, w_col, dist_gain, first_kernel, second_kernel, head_weight):
    channels = embedding.shape[1]
    operands = [
        embedding, bases_table, edit_pos.reshape(1, -1), edit_tok.reshape(1, -1), w_row, w_col,
        dist_gain.reshape(1, -1), first_kernel, second_kernel, head_weight.reshape(1, -1),
    ]
    turned = pl.pallas_call(
        kernel,
        out_shape=pltpu.VMEM((TILE_J, TILE_I), F32),
        in_specs=[pl.BlockSpec(memory_space=pltpu.HBM)] * 10,
        out_specs=pl.BlockSpec(memory_space=pltpu.VMEM),
        scratch_shapes=[
            pltpu.VMEM((32, channels), BF16),
            pltpu.VMEM((4, channels), BF16),
            pltpu.VMEM((1, 64), jnp.int32),
            pltpu.VMEM((1, 64), jnp.int32),
            pltpu.VMEM((channels, 2 * CH), BF16),
            pltpu.VMEM((1, CH), F32),
            pltpu.VMEM((1, CH), BF16),
            pltpu.VMEM((2, 4, 3, CH, 2 * CH), BF16),
            pltpu.VMEM((2, 4, 3, CH, 2 * CH), BF16),
            pltpu.VMEM((BINS, 2 * CH), BF16),
            pltpu.VMEM((10, BINS, 2 * CH), BF16),
            pltpu.VMEM((6, BINS, 2 * CH), BF16),
            pltpu.VMEM((LONG, 2 * CH), F32),
            pltpu.VMEM((48, 2 * CH), F32),
            pltpu.VMEM((128, CH), F32),
            pltpu.VMEM((PITCH, CH), F32),
            pltpu.VMEM((2, PAIR_J, PITCH, CH), BF16),
            pltpu.VMEM((2, PAIR_J, PITCH, CH), BF16),
            pltpu.VMEM((2, PAIR_J, PITCH, CH), BF16),
            pltpu.VMEM((2, HID_J, TILE_I, CH), BF16),
            pltpu.VMEM((2, HID_J, TILE_I, CH), BF16),
            pltpu.VMEM((2, HID_J, TILE_I, CH), BF16),
            pltpu.VMEM((8, LONG, CH), F32),
            pltpu.VMEM((8, PITCH, CH), F32),
            pltpu.SemaphoreType.DMA((32,)),
            pltpu.SemaphoreType.DMA((12,)),
            pltpu.SemaphoreType.DMA((1,)),
            pltpu.SemaphoreType.DMA((1,)),
            pltpu.SemaphoreType.DMA((1,)),
            pltpu.SemaphoreType.REGULAR((ROWS,)),
        ],
        compiler_params=pltpu.CompilerParams(
            collective_id=0, has_side_effects=True, vmem_limit_bytes=48 * 1024 * 1024
        ),
    )(*[pltpu.with_memory_space_constraint(x, pltpu.HBM) for x in operands])
    return turned.T


def solution(mesh):
    placed = (P(("row", "col"), None), P(), P("cand"), P("cand"), P(), P(), P(), P(), P(), P())
    return jax.shard_map(
        on_device, mesh=mesh, in_specs=placed, out_specs=P(("cand", "row"), "col"), check_vma=False
    )
```

```python
import math

import jax
import jax.numpy as jnp
from jax import lax
from jax.experimental import pallas as pl
from jax.experimental.pallas import tpu as pltpu
from jax.sharding import PartitionSpec as P

MESH = pl.DeviceIdType.MESH
BF16 = jnp.bfloat16
F32 = jnp.float32

ROWS, COLS = 4, 8
BINS = 8
POOL = 4
CH = 128
TILE_I, TILE_J = 64, 32
MAP = 256
LONG = 80
PITCH = 72
PAIR_J = 44
HID_J = 40
OUTSIDE = -1e30


def kernel(
    emb_h, tab_h, pos_h, tok_h, wr_h, wc_h, gain_h, k1_h, k2_h, hw_h,
    out_ref,
    emb, tab, pos, tok, w, gain, hw, rhs1, rhs2,
    proj, ibuf, jbuf, fi, fj, table, inside, x1a, x1b, x1c, x2a, x2b, x2c, moved, kept,
    in_sem, send_sem, i_sem, j_sem, block_sem, ready,
):
    r = lax.axis_index("row")
    c = lax.axis_index("col")
    g = r * COLS + c
    mine, part = g // 4, lax.rem(g, 4)
    left, right = mine - 1, mine + 1
    home = c // 2

    barrier = pltpu.get_barrier_semaphore()

    def tell(row, col):
        pl.semaphore_signal(barrier, inc=1, device_id={"row": row, "col": col}, device_id_type=MESH)

    for k in range(1, COLS):
        tell(r, lax.rem(c + k, COLS))

    @pl.when(home > r)
    def _():
        for k in range(5):
            tell((4 * c - 1 + k) // COLS, lax.rem(4 * c - 1 + k, COLS))

    @pl.when((home > r) & (c < COLS - 1))
    def _():
        tell((4 * c + 4) // COLS, lax.rem(4 * c + 4, COLS))

    def load(src, dst, k):
        copy = pltpu.make_async_copy(src, dst, in_sem.at[k])
        copy.start()
        return copy

    first = [load(emb_h, emb, 2), load(tab_h, tab, 3), load(pos_h, pos, 4), load(tok_h, tok, 5)]
    weights = [load(wr_h, w.at[:, pl.ds(0, CH)], 0), load(wc_h, w.at[:, pl.ds(CH, CH)], 1)]

    @pl.when(r > 0)
    def _():
        tell(r - 1, COLS - 1)

    @pl.when(r < ROWS - 1)
    def _():
        tell(r + 1, 0)

    for row in range(1, ROWS):
        @pl.when((home == r) & (row > r) & ((home > 0) | (row != 2)))
        def _():
            tell(row, c)

    @pl.when((home == 0) & (r == 1))
    def _():
        tell(2, c)

    for copy in first:
        copy.wait()
    own = lax.shift_right_logical(pos[...], 2) == g * BINS + lax.broadcasted_iota(jnp.int32, (BINS, 64), 0)
    token = jnp.broadcast_to(tok[...], (BINS, 64))
    pool = (
        lax.broadcasted_iota(jnp.int32, (BINS, 32), 1) // POOL == lax.broadcasted_iota(jnp.int32, (BINS, 32), 0)
    ).astype(BF16)
    total = jnp.dot(pool, emb[...], preferred_element_type=F32)
    bases = tab[...].astype(F32)
    for t in range(4):
        count = jnp.sum(jnp.where(own & (token == t), 1.0, 0.0), axis=1, keepdims=True)
        total = total + count * bases[t : t + 1, :]
    pooled = (total * (1.0 / POOL)).astype(BF16)
    for copy in weights:
        copy.wait()
    proj[...] = jnp.dot(pooled, w[...], preferred_element_type=F32).astype(BF16)

    has_left = (part == 0) & (mine > 0)
    has_right = (part == 3) & (mine < COLS - 1)
    is_top = (c == 0) & (r > 0)
    is_bottom = (c == COLS - 1) & (r < ROWS - 1)
    pl.semaphore_wait(
        barrier,
        COLS - 1 + r
        + jnp.where(has_left, left // 2, 0) + jnp.where(has_right, right // 2, 0)
        + jnp.where(is_top | is_bottom, COLS, 0) + jnp.where(home < r, 1, 0),
    )

    def send(src, dst, k, rsem, row, col):
        return pltpu.make_async_remote_copy(
            src_ref=src, dst_ref=dst, send_sem=send_sem.at[k], recv_sem=rsem,
            device_id={"row": row, "col": col}, device_id_type=MESH,
        )

    def j_send(k, slot, row, col):
        return send(proj, jbuf.at[slot], k, j_sem.at[0], row, col)

    def i_send(k, slot, row, col):
        send(proj, ibuf.at[slot], k, i_sem.at[0], row, col).start()

    def every_j_send(do):
        for row in range(ROWS - 1):
            @pl.when(has_left & (row < left // 2))
            def _():
                do(j_send(5 + row, 5, row, left))

        for row in range(ROWS - 1):
            @pl.when(has_right & (row < right // 2))
            def _():
                do(j_send(5 + row, 0, row, right))

        for row in range(ROWS - 1):
            @pl.when(row < r)
            def _():
                do(j_send(2 + row, part + 1, row, mine))

    def every_i_send():
        @pl.when(is_top)
        def _():
            for k in range(COLS):
                i_send(1, 9, r - 1, k)

        @pl.when(is_bottom)
        def _():
            for k in range(COLS):
                i_send(1, 0, r + 1, k)

        for k in range(1, COLS):
            i_send(0, c + 1, r, lax.rem(c + k, COLS))

    block = ibuf.at[pl.ds(4 * lax.rem(c, 2), 6)]
    source = jnp.where((home == 0) & (r == 2), 1, home)

    def forward(src, row):
        return send(src, jbuf, 8 + row, block_sem.at[0], row, c)

    def every_forward(do):
        for row in (1, 3, 2):
            @pl.when((home == r) & (row > r) & ((home > 0) | (row != 2)))
            def _():
                do(forward(block, row), row)

    relays = (home == 0) & (r == 1)

    every_j_send(lambda copy: copy.start())
    @pl.when(home < r)
    def _():
        pl.semaphore_signal(ready.at[r], inc=1, device_id={"row": source, "col": c}, device_id_type=MESH)

    every_i_send()


    later = [load(gain_h, gain, 6), load(hw_h, hw, 7)]
    for n, (source, rhs) in enumerate(((k1_h, rhs1), (k2_h, rhs2))):
        for b in range(3):
            for tile, taps in ((0, source.at[:, b]), (1, source.at[b])):
                at = 8 + 12 * n + 4 * b + 2 * tile
                later.append(load(taps, rhs.at[tile, b, :, :, pl.ds(0, CH)], at))
                later.append(load(taps, rhs.at[tile, b + 1, :, :, pl.ds(CH, CH)], at + 1))

    ibuf[c + 1] = proj[...]
    nothing = jnp.zeros((BINS, 2 * CH), BF16)

    @pl.when(r == 0)
    def _():
        ibuf[0] = nothing

    @pl.when(r == ROWS - 1)
    def _():
        ibuf[9] = nothing

    @pl.when((c == COLS - 1) & (home > r))
    def _():
        jbuf[5] = nothing

    blank = jnp.zeros((3, CH, CH), BF16)
    for rhs in (rhs1, rhs2):
        for tile in range(2):
            rhs[tile, 3, :, :, pl.ds(0, CH)] = blank
            rhs[tile, 0, :, :, pl.ds(CH, CH)] = blank
    for copy in later:
        copy.wait()
    offset = (TILE_I * r - TILE_J * c - 43 + lax.broadcasted_iota(jnp.int32, (128, CH), 0)).astype(F32)
    table[...] = gain[...] * (jnp.log(1.0 + jnp.abs(offset)) * (1.0 / math.log(MAP)))
    bin_i = TILE_I * r - 4 + lax.broadcasted_iota(jnp.int32, (PITCH, CH), 0)
    inside[...] = ((bin_i >= 0) & (bin_i < MAP)).astype(F32)
    head = jnp.broadcast_to(hw[...].astype(F32), (CH, CH)).T.astype(BF16)
    lane = lax.broadcasted_iota(jnp.int32, (TILE_I, CH), 1)

    def arrived(buf, count, sem):
        some = buf.at[pl.ds(0, count)]
        pltpu.make_async_copy(some, some, sem.at[0]).wait()

    inner = (r > 0) & (r < ROWS - 1)

    @pl.when(inner)
    def _():
        arrived(ibuf, COLS + 1, i_sem)

    @pl.when(jnp.logical_not(inner))
    def _():
        arrived(ibuf, COLS, i_sem)

    def forward_now(copy, row):
        pl.semaphore_wait(ready.at[row], 1)
        copy.start()

    every_forward(forward_now)

    def fill(out, at, block, start, size):
        bins = start + lax.broadcasted_iota(jnp.int32, (size, 2 * CH), 0)
        values = block.astype(F32).reshape(size, 2 * CH)
        out[pl.ds(at, size), :] = jnp.where((bins >= 0) & (bins < MAP), values, OUTSIDE)

    fill(fi, 0, ibuf[...], TILE_I * r - 8, LONG)

    @pl.when(home == r)
    def _():
        fill(fj, 0, ibuf[pl.ds(4 * lax.rem(c, 2), 6)], TILE_J * c - 8, 48)

    @pl.when((home > r) & (c < COLS - 1))
    def _():
        arrived(jbuf, 6, j_sem)

    @pl.when((home > r) & (c == COLS - 1))
    def _():
        arrived(jbuf, 5, j_sem)

    @pl.when(home < r)
    def _():
        arrived(jbuf, 6, block_sem)

    @pl.when(relays)
    def _():
        forward_now(forward(jbuf, 2), 2)

    @pl.when(home != r)
    def _():
        fill(fj, 0, jbuf[...], TILE_J * c - 8, 48)

    def sent(count, k):
        some = ibuf.at[pl.ds(0, count)]
        pltpu.make_async_copy(some, some, send_sem.at[k]).wait()

    sent(COLS - 1, 0)

    @pl.when(is_top | is_bottom)
    def _():
        sent(COLS, 1)

    every_j_send(lambda copy: copy.wait_send())

    x1, x2 = (x1a, x1b, x1c), (x2a, x2b, x2c)

    def pair_maps(first, end):
        for p in range(first, end):
            far = table[pl.ds(43 - p, PITCH + 4), :]
            for tile in range(2):
                side = fi[pl.ds(2, PITCH + 4), pl.ds(tile * CH, CH)]
                value = jnp.maximum(side + fj[pl.ds(p + 2, 1), pl.ds((1 - tile) * CH, CH)] + far, 0.0)
                slot = (2 * p + tile) % 8
                moved[slot, pl.ds(0, PITCH + 4), :] = value
                x1[0][tile, p] = value[:PITCH].astype(BF16)
                for a in (1, 2):
                    x1[a][tile, p] = moved[slot, pl.ds(2 * a, PITCH), :].astype(BF16)

    top, bottom = inside[pl.ds(0, 8), :], inside[pl.ds(PITCH - 8, 8), :]

    def first_conv(n):
        starts = [8 * n + s for s in (0, 1, 4, 5)]
        for tile in range(2):
            lhs = jnp.concatenate(
                [jnp.concatenate([x1[a][tile, q + 2 * m] for m in range(4) for a in range(3)], axis=1) for q in starts], axis=0
            )
            acc = jnp.dot(lhs, rhs1[tile].reshape(12 * CH, 2 * CH), preferred_element_type=F32)
            for k in range(4):
                for half in range(2):
                    q = starts[k] + 2 * half
                    conv = jnp.maximum(acc[PITCH * k : PITCH * (k + 1), CH * half : CH * (half + 1)], 0.0)
                    conv = jnp.concatenate([conv[:8] * top, conv[8 : PITCH - 8], conv[PITCH - 8 :] * bottom], axis=0)
                    if q < 4:
                        conv = conv * jnp.where(c > 0, 1.0, 0.0)
                    if q >= HID_J - 4:
                        conv = conv * jnp.where(c < COLS - 1, 1.0, 0.0)
                    hidden = x1[1][tile, q + 2].astype(F32) + conv
                    kept[q % 8] = hidden
                    x2[0][tile, q] = hidden[:TILE_I].astype(BF16)
                    x2[1][tile, q] = kept[q % 8, pl.ds(4, TILE_I), :].astype(BF16)
                    x2[2][tile, q] = hidden[8:].astype(BF16)

    def second_conv(n, total):
        t0 = 8 * n
        accs = []
        for tile in range(2):
            lhs = jnp.concatenate(
                [jnp.concatenate([x2[a][tile, t0 + s + 4 * m] for m in range(4) for a in range(3)], axis=1) for s in range(4)], axis=0
            )
            accs.append(jnp.dot(lhs, rhs2[tile].reshape(12 * CH, 2 * CH), preferred_element_type=F32))
        pieces = []
        for half in range(2):
            for s in range(4):
                hidden = 0.0
                for tile in range(2):
                    conv = accs[tile][TILE_I * s : TILE_I * (s + 1), CH * half : CH * (half + 1)]
                    base = x2[1][tile, t0 + s + 4 * half + 4].astype(F32)
                    hidden = hidden + (base + jnp.maximum(conv, 0.0))
                pieces.append(hidden.astype(BF16))
        points = jnp.dot(jnp.concatenate(pieces, axis=0), head, preferred_element_type=F32)
        for k in range(8):
            total = jnp.where(lane == t0 + k, points[TILE_I * k : TILE_I * (k + 1)], total)
        return total

    total = jnp.zeros((TILE_I, CH), F32)
    pair_maps(0, 12)
    for n in range(HID_J // 8):
        pair_maps(8 * n + 12, min(8 * n + 20, PAIR_J))
        first_conv(n)
        if n > 0:
            total = second_conv(n - 1, total)
    out_ref[...] = 0.5 * total.T[:TILE_J]

    every_forward(lambda copy, row: copy.wait_send())

    @pl.when(relays)
    def _():
        forward(jbuf, 2).wait_send()


def on_device(embedding, bases_table, edit_pos, edit_tok, w_row, w_col, dist_gain, first_kernel, second_kernel, head_weight):
    channels = embedding.shape[1]
    operands = [
        embedding, bases_table, edit_pos.reshape(1, -1), edit_tok.reshape(1, -1), w_row, w_col,
        dist_gain.reshape(1, -1), first_kernel, second_kernel, head_weight.reshape(1, -1),
    ]
    turned = pl.pallas_call(
        kernel,
        out_shape=pltpu.VMEM((TILE_J, TILE_I), F32),
        in_specs=[pl.BlockSpec(memory_space=pltpu.HBM)] * 10,
        out_specs=pl.BlockSpec(memory_space=pltpu.VMEM),
        scratch_shapes=[
            pltpu.VMEM((32, channels), BF16),
            pltpu.VMEM((4, channels), BF16),
            pltpu.VMEM((1, 64), jnp.int32),
            pltpu.VMEM((1, 64), jnp.int32),
            pltpu.VMEM((channels, 2 * CH), BF16),
            pltpu.VMEM((1, CH), F32),
            pltpu.VMEM((1, CH), BF16),
            pltpu.VMEM((2, 4, 3, CH, 2 * CH), BF16),
            pltpu.VMEM((2, 4, 3, CH, 2 * CH), BF16),
            pltpu.VMEM((BINS, 2 * CH), BF16),
            pltpu.VMEM((10, BINS, 2 * CH), BF16),
            pltpu.VMEM((6, BINS, 2 * CH), BF16),
            pltpu.VMEM((LONG, 2 * CH), F32),
            pltpu.VMEM((48, 2 * CH), F32),
            pltpu.VMEM((128, CH), F32),
            pltpu.VMEM((PITCH, CH), F32),
            pltpu.VMEM((2, PAIR_J, PITCH, CH), BF16),
            pltpu.VMEM((2, PAIR_J, PITCH, CH), BF16),
            pltpu.VMEM((2, PAIR_J, PITCH, CH), BF16),
            pltpu.VMEM((2, HID_J, TILE_I, CH), BF16),
            pltpu.VMEM((2, HID_J, TILE_I, CH), BF16),
            pltpu.VMEM((2, HID_J, TILE_I, CH), BF16),
            pltpu.VMEM((8, LONG, CH), F32),
            pltpu.VMEM((8, PITCH, CH), F32),
            pltpu.SemaphoreType.DMA((32,)),
            pltpu.SemaphoreType.DMA((12,)),
            pltpu.SemaphoreType.DMA((1,)),
            pltpu.SemaphoreType.DMA((1,)),
            pltpu.SemaphoreType.DMA((1,)),
            pltpu.SemaphoreType.REGULAR((ROWS,)),
        ],
        compiler_params=pltpu.CompilerParams(
            collective_id=0, has_side_effects=True, vmem_limit_bytes=48 * 1024 * 1024
        ),
    )(*[pltpu.with_memory_space_constraint(x, pltpu.HBM) for x in operands])
    return turned.T


def solution(mesh):
    placed = (P(("row", "col"), None), P(), P("cand"), P("cand"), P(), P(), P(), P(), P(), P())
    return jax.shard_map(
        on_device, mesh=mesh, in_specs=placed, out_specs=P(("cand", "row"), "col"), check_vma=False
    )
```

```python
import math

import jax
import jax.numpy as jnp
from jax import lax
from jax.experimental import pallas as pl
from jax.experimental.pallas import tpu as pltpu
from jax.sharding import PartitionSpec as P

MESH = pl.DeviceIdType.MESH
BF16 = jnp.bfloat16
F32 = jnp.float32

ROWS, COLS = 4, 8
BINS = 8
POOL = 4
CH = 128
TILE_I, TILE_J = 64, 32
MAP = 256
LONG = 80
PITCH = 72
PAIR_J = 44
HID_J = 40
OUTSIDE = -1e30


def kernel(
    emb_h, tab_h, pos_h, tok_h, wr_h, wc_h, gain_h, k1_h, k2_h, hw_h,
    out_ref,
    emb, tab, pos, tok, w, gain, hw, rhs1, rhs2,
    proj, ibuf, jbuf, fi, fj, table, inside, x1a, x1b, x1c, x2a, x2b, x2c, moved, kept,
    in_sem, send_sem, i_sem, j_sem, block_sem, ready,
):
    r = lax.axis_index("row")
    c = lax.axis_index("col")
    g = r * COLS + c
    mine, part = g // 4, lax.rem(g, 4)
    left, right = mine - 1, mine + 1
    home = c // 2

    barrier = pltpu.get_barrier_semaphore()

    def tell(row, col):
        pl.semaphore_signal(barrier, inc=1, device_id={"row": row, "col": col}, device_id_type=MESH)

    for k in range(1, COLS):
        tell(r, lax.rem(c + k, COLS))

    @pl.when(home > r)
    def _():
        for k in range(5):
            tell((4 * c - 1 + k) // COLS, lax.rem(4 * c - 1 + k, COLS))

    @pl.when((home > r) & (c < COLS - 1))
    def _():
        tell((4 * c + 4) // COLS, lax.rem(4 * c + 4, COLS))

    def load(src, dst, k):
        copy = pltpu.make_async_copy(src, dst, in_sem.at[k])
        copy.start()
        return copy

    first = [load(emb_h, emb, 2), load(tab_h, tab, 3), load(pos_h, pos, 4), load(tok_h, tok, 5)]
    weights = [load(wr_h, w.at[:, pl.ds(0, CH)], 0), load(wc_h, w.at[:, pl.ds(CH, CH)], 1)]

    @pl.when(r > 0)
    def _():
        tell(r - 1, COLS - 1)

    @pl.when(r < ROWS - 1)
    def _():
        tell(r + 1, 0)

    for row in range(1, ROWS):
        @pl.when((home == r) & (row > r) & ((home > 0) | (row != 2)))
        def _():
            tell(row, c)

    @pl.when((home == 0) & (r == 1))
    def _():
        tell(2, c)

    for copy in first:
        copy.wait()
    own = lax.shift_right_logical(pos[...], 2) == g * BINS + lax.broadcasted_iota(jnp.int32, (BINS, 64), 0)
    token = jnp.broadcast_to(tok[...], (BINS, 64))
    pool = (
        lax.broadcasted_iota(jnp.int32, (BINS, 32), 1) // POOL == lax.broadcasted_iota(jnp.int32, (BINS, 32), 0)
    ).astype(BF16)
    total = jnp.dot(pool, emb[...], preferred_element_type=F32)
    bases = tab[...].astype(F32)
    for t in range(4):
        count = jnp.sum(jnp.where(own & (token == t), 1.0, 0.0), axis=1, keepdims=True)
        total = total + count * bases[t : t + 1, :]
    pooled = (total * (1.0 / POOL)).astype(BF16)
    for copy in weights:
        copy.wait()
    proj[...] = jnp.dot(pooled, w[...], preferred_element_type=F32).astype(BF16)

    has_left = (part == 0) & (mine > 0)
    has_right = (part == 3) & (mine < COLS - 1)
    is_top = (c == 0) & (r > 0)
    is_bottom = (c == COLS - 1) & (r < ROWS - 1)
    pl.semaphore_wait(
        barrier,
        COLS - 1 + r
        + jnp.where(has_left, left // 2, 0) + jnp.where(has_right, right // 2, 0)
        + jnp.where(is_top | is_bottom, COLS, 0) + jnp.where(home < r, 1, 0),
    )

    def send(src, dst, k, rsem, row, col):
        return pltpu.make_async_remote_copy(
            src_ref=src, dst_ref=dst, send_sem=send_sem.at[k], recv_sem=rsem,
            device_id={"row": row, "col": col}, device_id_type=MESH,
        )

    def j_send(k, slot, row, col):
        return send(proj, jbuf.at[slot], k, j_sem.at[0], row, col)

    def i_send(k, slot, row, col):
        send(proj, ibuf.at[slot], k, i_sem.at[0], row, col).start()

    def every_j_send(do):
        for row in range(ROWS - 1):
            @pl.when(has_left & (row < left // 2))
            def _():
                do(j_send(5 + row, 5, row, left))

        for row in range(ROWS - 1):
            @pl.when(has_right & (row < right // 2))
            def _():
                do(j_send(5 + row, 0, row, right))

        for row in range(ROWS - 1):
            @pl.when(row < r)
            def _():
                do(j_send(2 + row, part + 1, row, mine))

    def every_i_send():
        @pl.when(is_top)
        def _():
            for k in range(COLS):
                i_send(1, 9, r - 1, k)

        @pl.when(is_bottom)
        def _():
            for k in range(COLS):
                i_send(1, 0, r + 1, k)

        for k in range(1, COLS):
            i_send(0, c + 1, r, lax.rem(c + k, COLS))

    block = ibuf.at[pl.ds(4 * lax.rem(c, 2), 6)]
    source = jnp.where((home == 0) & (r == 2), 1, home)

    def forward(src, row):
        return send(src, jbuf, 8 + row, block_sem.at[0], row, c)

    def every_forward(do):
        for row in (1, 3, 2):
            @pl.when((home == r) & (row > r) & ((home > 0) | (row != 2)))
            def _():
                do(forward(block, row), row)

    relays = (home == 0) & (r == 1)

    every_j_send(lambda copy: copy.start())
    @pl.when(home < r)
    def _():
        pl.semaphore_signal(ready.at[r], inc=1, device_id={"row": source, "col": c}, device_id_type=MESH)

    every_i_send()


    later = [load(gain_h, gain, 6), load(hw_h, hw, 7)]
    for n, (source, rhs) in enumerate(((k1_h, rhs1), (k2_h, rhs2))):
        for b in range(3):
            for tile, taps in ((0, source.at[:, b]), (1, source.at[b])):
                at = 8 + 12 * n + 4 * b + 2 * tile
                later.append(load(taps, rhs.at[tile, b, :, :, pl.ds(0, CH)], at))
                later.append(load(taps, rhs.at[tile, b + 1, :, :, pl.ds(CH, CH)], at + 1))

    ibuf[c + 1] = proj[...]
    nothing = jnp.zeros((BINS, 2 * CH), BF16)

    @pl.when(r == 0)
    def _():
        ibuf[0] = nothing

    @pl.when(r == ROWS - 1)
    def _():
        ibuf[9] = nothing

    @pl.when((c == COLS - 1) & (home > r))
    def _():
        jbuf[5] = nothing

    blank = jnp.zeros((3, CH, CH), BF16)
    for rhs in (rhs1, rhs2):
        for tile in range(2):
            rhs[tile, 3, :, :, pl.ds(0, CH)] = blank
            rhs[tile, 0, :, :, pl.ds(CH, CH)] = blank
    for copy in later:
        copy.wait()
    offset = (TILE_I * r - TILE_J * c - 43 + lax.broadcasted_iota(jnp.int32, (128, CH), 0)).astype(F32)
    table[...] = gain[...] * (jnp.log(1.0 + jnp.abs(offset)) * (1.0 / math.log(MAP)))
    bin_i = TILE_I * r - 4 + lax.broadcasted_iota(jnp.int32, (PITCH, CH), 0)
    inside[...] = ((bin_i >= 0) & (bin_i < MAP)).astype(F32)
    head = jnp.broadcast_to(hw[...].astype(F32), (CH, CH)).T.astype(BF16)
    lane = lax.broadcasted_iota(jnp.int32, (TILE_I, CH), 1)

    def arrived(buf, count, sem):
        some = buf.at[pl.ds(0, count)]
        pltpu.make_async_copy(some, some, sem.at[0]).wait()

    inner = (r > 0) & (r < ROWS - 1)

    @pl.when(inner)
    def _():
        arrived(ibuf, COLS + 1, i_sem)

    @pl.when(jnp.logical_not(inner))
    def _():
        arrived(ibuf, COLS, i_sem)

    def forward_now(copy, row):
        pl.semaphore_wait(ready.at[row], 1)
        copy.start()

    every_forward(forward_now)

    def fill(out, at, block, start, size):
        bins = start + lax.broadcasted_iota(jnp.int32, (size, 2 * CH), 0)
        values = block.astype(F32).reshape(size, 2 * CH)
        out[pl.ds(at, size), :] = jnp.where((bins >= 0) & (bins < MAP), values, OUTSIDE)

    fill(fi, 0, ibuf[...], TILE_I * r - 8, LONG)

    @pl.when(home == r)
    def _():
        fill(fj, 0, ibuf[pl.ds(4 * lax.rem(c, 2), 6)], TILE_J * c - 8, 48)

    @pl.when((home > r) & (c < COLS - 1))
    def _():
        arrived(jbuf, 6, j_sem)

    @pl.when((home > r) & (c == COLS - 1))
    def _():
        arrived(jbuf, 5, j_sem)

    @pl.when(home < r)
    def _():
        arrived(jbuf, 6, block_sem)

    @pl.when(relays)
    def _():
        forward_now(forward(jbuf, 2), 2)

    @pl.when(home != r)
    def _():
        fill(fj, 0, jbuf[...], TILE_J * c - 8, 48)

    def sent(count, k):
        some = ibuf.at[pl.ds(0, count)]
        pltpu.make_async_copy(some, some, send_sem.at[k]).wait()

    sent(COLS - 1, 0)

    @pl.when(is_top | is_bottom)
    def _():
        sent(COLS, 1)

    every_j_send(lambda copy: copy.wait_send())

    x1, x2 = (x1a, x1b, x1c), (x2a, x2b, x2c)

    def pair_maps(first, end):
        for p in range(first, end):
            far = table[pl.ds(43 - p, PITCH + 4), :]
            for tile in range(2):
                side = fi[pl.ds(2, PITCH + 4), pl.ds(tile * CH, CH)]
                value = jnp.maximum(side + fj[pl.ds(p + 2, 1), pl.ds((1 - tile) * CH, CH)] + far, 0.0)
                slot = (2 * p + tile) % 32
                moved[slot, pl.ds(0, PITCH + 4), :] = value
                x1[0][tile, p] = value[:PITCH].astype(BF16)
                for a in (1, 2):
                    x1[a][tile, p] = moved[slot, pl.ds(2 * a, PITCH), :].astype(BF16)

    top, bottom = inside[pl.ds(0, 8), :], inside[pl.ds(PITCH - 8, 8), :]

    def first_conv(n):
        starts = [8 * n + s for s in (0, 1, 4, 5)]
        for tile in range(2):
            lhs = jnp.concatenate(
                [jnp.concatenate([x1[a][tile, q + 2 * m] for m in range(4) for a in range(3)], axis=1) for q in starts], axis=0
            )
            acc = jnp.dot(lhs, rhs1[tile].reshape(12 * CH, 2 * CH), preferred_element_type=F32)
            for k in range(4):
                for half in range(2):
                    q = starts[k] + 2 * half
                    conv = jnp.maximum(acc[PITCH * k : PITCH * (k + 1), CH * half : CH * (half + 1)], 0.0)
                    conv = jnp.concatenate([conv[:8] * top, conv[8 : PITCH - 8], conv[PITCH - 8 :] * bottom], axis=0)
                    if q < 4:
                        conv = conv * jnp.where(c > 0, 1.0, 0.0)
                    if q >= HID_J - 4:
                        conv = conv * jnp.where(c < COLS - 1, 1.0, 0.0)
                    hidden = x1[1][tile, q + 2].astype(F32) + conv
                    kept[2 * (q % 16) + tile] = hidden
                    x2[0][tile, q] = hidden[:TILE_I].astype(BF16)
                    x2[1][tile, q] = kept[2 * (q % 16) + tile, pl.ds(4, TILE_I), :].astype(BF16)
                    x2[2][tile, q] = hidden[8:].astype(BF16)

    def second_conv(n, total):
        t0 = 8 * n
        accs = []
        for tile in range(2):
            lhs = jnp.concatenate(
                [jnp.concatenate([x2[a][tile, t0 + s + 4 * m] for m in range(4) for a in range(3)], axis=1) for s in range(4)], axis=0
            )
            accs.append(jnp.dot(lhs, rhs2[tile].reshape(12 * CH, 2 * CH), preferred_element_type=F32))
        pieces = []
        for half in range(2):
            for s in range(4):
                hidden = 0.0
                for tile in range(2):
                    conv = accs[tile][TILE_I * s : TILE_I * (s + 1), CH * half : CH * (half + 1)]
                    base = x2[1][tile, t0 + s + 4 * half + 4].astype(F32)
                    hidden = hidden + (base + jnp.maximum(conv, 0.0))
                pieces.append(hidden.astype(BF16))
        points = jnp.dot(jnp.concatenate(pieces, axis=0), head, preferred_element_type=F32)
        for k in range(8):
            total = jnp.where(lane == t0 + k, points[TILE_I * k : TILE_I * (k + 1)], total)
        return total

    total = jnp.zeros((TILE_I, CH), F32)
    pair_maps(0, 12)
    for n in range(HID_J // 8):
        pair_maps(8 * n + 12, min(8 * n + 20, PAIR_J))
        first_conv(n)
        if n > 0:
            total = second_conv(n - 1, total)
    out_ref[...] = 0.5 * total.T[:TILE_J]

    every_forward(lambda copy, row: copy.wait_send())

    @pl.when(relays)
    def _():
        forward(jbuf, 2).wait_send()


def on_device(embedding, bases_table, edit_pos, edit_tok, w_row, w_col, dist_gain, first_kernel, second_kernel, head_weight):
    channels = embedding.shape[1]
    operands = [
        embedding, bases_table, edit_pos.reshape(1, -1), edit_tok.reshape(1, -1), w_row, w_col,
        dist_gain.reshape(1, -1), first_kernel, second_kernel, head_weight.reshape(1, -1),
    ]
    turned = pl.pallas_call(
        kernel,
        out_shape=pltpu.VMEM((TILE_J, TILE_I), F32),
        in_specs=[pl.BlockSpec(memory_space=pltpu.HBM)] * 10,
        out_specs=pl.BlockSpec(memory_space=pltpu.VMEM),
        scratch_shapes=[
            pltpu.VMEM((32, channels), BF16),
            pltpu.VMEM((4, channels), BF16),
            pltpu.VMEM((1, 64), jnp.int32),
            pltpu.VMEM((1, 64), jnp.int32),
            pltpu.VMEM((channels, 2 * CH), BF16),
            pltpu.VMEM((1, CH), F32),
            pltpu.VMEM((1, CH), BF16),
            pltpu.VMEM((2, 4, 3, CH, 2 * CH), BF16),
            pltpu.VMEM((2, 4, 3, CH, 2 * CH), BF16),
            pltpu.VMEM((BINS, 2 * CH), BF16),
            pltpu.VMEM((10, BINS, 2 * CH), BF16),
            pltpu.VMEM((6, BINS, 2 * CH), BF16),
            pltpu.VMEM((LONG, 2 * CH), F32),
            pltpu.VMEM((48, 2 * CH), F32),
            pltpu.VMEM((128, CH), F32),
            pltpu.VMEM((PITCH, CH), F32),
            pltpu.VMEM((2, PAIR_J, PITCH, CH), BF16),
            pltpu.VMEM((2, PAIR_J, PITCH, CH), BF16),
            pltpu.VMEM((2, PAIR_J, PITCH, CH), BF16),
            pltpu.VMEM((2, HID_J, TILE_I, CH), BF16),
            pltpu.VMEM((2, HID_J, TILE_I, CH), BF16),
            pltpu.VMEM((2, HID_J, TILE_I, CH), BF16),
            pltpu.VMEM((32, LONG, CH), F32),
            pltpu.VMEM((32, PITCH, CH), F32),
            pltpu.SemaphoreType.DMA((32,)),
            pltpu.SemaphoreType.DMA((12,)),
            pltpu.SemaphoreType.DMA((1,)),
            pltpu.SemaphoreType.DMA((1,)),
            pltpu.SemaphoreType.DMA((1,)),
            pltpu.SemaphoreType.REGULAR((ROWS,)),
        ],
        compiler_params=pltpu.CompilerParams(
            collective_id=0, has_side_effects=True, vmem_limit_bytes=48 * 1024 * 1024
        ),
    )(*[pltpu.with_memory_space_constraint(x, pltpu.HBM) for x in operands])
    return turned.T


def solution(mesh):
    placed = (P(("row", "col"), None), P(), P("cand"), P("cand"), P(), P(), P(), P(), P(), P())
    return jax.shard_map(
        on_device, mesh=mesh, in_specs=placed, out_specs=P(("cand", "row"), "col"), check_vma=False
    )
```
